32 devices in a mesh: dp: 16 (over z, y, x), section: 2 (over core).
Axes of the slice: x: 2, y: 2, z: 4, core: 2. Of those that a mesh axis runs over, the one named last changes fastest.
Arguments:
- acts: bfloat16 [2, 2, 2048, 2048], P('section', None, 'dp'), may hold values from -6 to 6
- cotan: bfloat16 [2, 2, 2048, 384], P('section', None, 'dp'), may hold values from -0.09375 to 0.09375
- counts: int32 [2, 2, 16, 1], P('section', None, 'dp'), may hold values from 32 to 128
- weight: float32 [2, 786432], P('section', 'dp'), may hold values from -4 to 4
- moment: float32 [2, 786432], P('section', 'dp'), may hold values from -4 to 4
- second: float32 [2, 786432], P('section', 'dp'), may hold values from 0.1 to 1
Outputs:
- new_weight: float32 [2, 786432], P('section', 'dp')
- new_moment: float32 [2, 786432], P('section', 'dp')
- new_second: float32 [2, 786432], P('section', 'dp')
The draws below stay inside these ranges and needn't reach their ends.
All inputs are finite; a program needn't handle non-finite values.
Results may differ from the reference program's by a relative error of at most 0.0003.
Values sent between devices are 32-bit elements; how exact they have to be, the bound alone decides.
A program may use at most 64 MiB of HBM per device.

```python
import math
import jax
import jax.numpy as jnp
from jax import lax

D = 2048
F = 384
CAP = 128
MICRO = 1
ROWS_ALL = 2048
SECTIONS = 2
FLAT = 786432
N_DP = 16


def set_ends(result, own_key, least, top_value):
    index_at = [jax.random.randint(jax.random.fold_in(own_key, axis), (), 0, length) for axis, length in enumerate(result.shape)]
    main_axis = result.shape.index(max(result.shape))
    neighbour = index_at[:main_axis] + [(index_at[main_axis] + 1) % result.shape[main_axis]] + index_at[main_axis + 1:]
    return result.at[tuple(index_at)].set(least).at[tuple(neighbour)].set(top_value)


def levels(own_key, shape, split, low, high):
    level = 1.0
    for axis_at, parts in split:
        heights = jax.random.uniform(jax.random.fold_in(jax.random.fold_in(own_key, 6), axis_at), (parts,), jnp.float32, low / len(split), high / len(split))
        level = level * jnp.repeat(jnp.exp(heights), shape[axis_at] // parts).reshape((-1,) + (1,) * (len(shape) - 1 - axis_at))
    return level


def normal_values(stream_key, extent, width, reach, pieces=(), held_as=jnp.bfloat16):
    drawn = jax.random.normal(stream_key, extent, jnp.float32) * width
    if len(pieces) > 0:
        drawn = levels(stream_key, extent, pieces, -0.22, 0.18) * drawn
    return jnp.clip(drawn, min=-reach, max=reach).astype(held_as)


def setup_inputs(seed: int = 0) -> dict:
    key_of = jax.random.split(jax.random.key(seed), 7)
    return {
        "acts": normal_values(key_of[0], (SECTIONS, 2, ROWS_ALL, D), 1.0, 6.0, ((0, 2), (2, 16))),
        "cotan": normal_values(key_of[1], (SECTIONS, 2, ROWS_ALL, F), (2 * ROWS_ALL) ** -0.5, 0.09375, ((0, 2), (2, 16))),
        "counts": set_ends(jax.random.randint(key_of[2], (SECTIONS, 2, N_DP, MICRO), CAP // 4, CAP + 1), jax.random.fold_in(key_of[2], 1), CAP // 4, CAP).astype(jnp.int32),
        "weight": normal_values(key_of[3], (SECTIONS, FLAT), 0.5, 4.0, ((0, 2), (1, 16)), jnp.float32),
        "moment": normal_values(key_of[4], (SECTIONS, FLAT), 0.5, 4.0, ((0, 2), (1, 16)), jnp.float32),
        "second": jnp.clip(jnp.exp(math.log(1.0) - 2.3025851 * jax.random.uniform(key_of[5], (SECTIONS, FLAT), jnp.float32) ** levels(key_of[5], (SECTIONS, FLAT), ((0, 2), (1, 16)), -0.2, 0.2)), 0.1, 1.0),
    }


def layer_grad(acts_dir, cotan_dir, live_dir):
    blocks_a = acts_dir.reshape(N_DP, -1, acts_dir.shape[-1])
    blocks_c = cotan_dir.reshape(N_DP, -1, cotan_dir.shape[-1])
    blocks_m = live_dir.reshape(N_DP, -1)

    def step(carry, item):
        block_a, block_c, block_m = item
        masked = block_c * block_m[:, None].astype(jnp.bfloat16)
        term = jnp.einsum('rd,rf->df', block_a.astype(jnp.float32), masked.astype(jnp.float32), precision=lax.Precision.HIGHEST)
        return (carry + term, None)
    start = jnp.zeros((acts_dir.shape[-1], cotan_dir.shape[-1]), jnp.float32)
    total, unused = lax.scan(step, start, (blocks_a, blocks_c, blocks_m))
    return total

def reference(acts, cotan, counts, weight, moment, second):
    slot = lax.broadcasted_iota(jnp.int32, (MICRO, CAP), 1)
    live = (slot[None, None, None] < counts[..., None]).reshape(SECTIONS, 2, ROWS_ALL)
    outs_w, outs_m, outs_v = ([], [], [])
    for layer in range(SECTIONS):
        other = SECTIONS - 1 - layer
        grad = layer_grad(acts[layer, 0], cotan[layer, 0], live[layer, 0]) + layer_grad(acts[other, 1], cotan[other, 1], live[other, 1])
        grad = grad.reshape(-1)
        new_m = 0.9 * moment[layer] + 0.1 * grad
        new_v = 0.95 * second[layer] + 0.05 * grad * grad
        corr_m = new_m / (1.0 - 0.9 ** 10)
        corr_v = new_v / (1.0 - 0.95 ** 10)
        new_w = weight[layer] - 0.01 * (corr_m / (jnp.sqrt(corr_v) + 1e-08) + 0.1 * weight[layer])
        outs_w.append(new_w)
        outs_m.append(new_m)
        outs_v.append(new_v)
    return (jnp.stack(outs_w), jnp.stack(outs_m), jnp.stack(outs_v))
```

```python
import functools
import jax
import jax.numpy as jnp
from jax import lax
from jax.experimental import pallas as pl
from jax.experimental.pallas import tpu as pltpu
from jax.sharding import PartitionSpec as P

LANES = 128
MESH = pl.DeviceIdType.MESH


CHUNKS = {"A": (7,), "B": (7,), "C": (1,), "D": (1,)}
FINALS = (("C", 0), ("D", 0), ("A", 0), ("B", 0))
ORDERS = (
    (
        ("1", "A", 0, 1, 3), ("1", "B", 0, 1, 3), ("z", "C", 0, 1, 1, 3), ("z", "D", 0, 1, 1, 3), ("z", "C", 0, 1, 1, 2),
        ("z", "D", 0, 1, 1, 2), ("z", "C", 0, 1, 1, 1), ("z", "C", 0, 0, 1, 3), ("z", "C", 0, 1, 0, 3), ("1", "A", 0, 1, 2),
        ("1", "A", 0, 1, 1), ("1", "B", 0, 1, 2), ("z", "D", 0, 0, 1, 3), ("z", "D", 0, 1, 0, 3), ("z", "C", 0, 0, 1, 2),
        ("z", "C", 0, 1, 0, 2), ("z", "D", 0, 1, 1, 1), ("z", "C", 0, 0, 0, 3), ("z", "D", 0, 0, 1, 2), ("1", "B", 0, 1, 1),
        ("1", "B", 0, 0, 3), ("z", "D", 0, 1, 0, 2), ("z", "D", 0, 0, 0, 3), ("z", "C", 0, 0, 1, 1), ("z", "C", 0, 1, 0, 1),
        ("z", "C", 0, 0, 0, 2), ("z", "D", 0, 0, 1, 1), ("z", "D", 0, 1, 0, 1), ("1", "A", 0, 0, 3), ("2", "B", 0, 3),
        ("z", "D", 0, 0, 0, 2), ("z", "C", 0, 0, 0, 1), ("z", "D", 0, 0, 0, 1), ("2", "A", 0, 3), ("1", "A", 0, 0, 2),
        ("2", "B", 0, 2), ("2", "A", 0, 2), ("1", "B", 0, 0, 2), ("3", "B", 0, 3), ("1", "A", 0, 1, 0), ("1", "A", 0, 0, 1),
        ("2", "A", 0, 1), ("3", "A", 0, 3), ("1", "B", 0, 1, 0), ("3", "A", 0, 2), ("2", "B", 0, 1), ("x", "C", 0, 1),
        ("1", "B", 0, 0, 1), ("3", "B", 0, 2), ("x", "D", 0, 1), ("1", "A", 0, 0, 0), ("x", "C", 0, 0), ("2", "A", 0, 0),
        ("3", "A", 0, 1), ("1", "B", 0, 0, 0), ("2", "B", 0, 0), ("3", "B", 0, 1), ("y", "C", 0), ("y", "D", 0),
        ("x", "D", 0, 0),
    ),
    (
        ("1", "A", 0, 1, 3), ("1", "B", 0, 1, 3), ("1", "A", 0, 1, 0), ("1", "A", 0, 1, 2), ("1", "B", 0, 1, 0),
        ("z", "C", 0, 1, 1, 3), ("z", "D", 0, 1, 1, 3), ("z", "C", 0, 1, 1, 2), ("z", "D", 0, 1, 1, 2), ("1", "B", 0, 1, 2),
        ("z", "C", 0, 0, 1, 3), ("z", "C", 0, 1, 0, 3), ("z", "D", 0, 0, 1, 3), ("z", "D", 0, 1, 0, 3), ("z", "C", 0, 0, 1, 2),
        ("z", "C", 0, 1, 0, 2), ("1", "A", 0, 0, 3), ("2", "B", 0, 3), ("2", "A", 0, 3), ("z", "C", 0, 0, 0, 3),
        ("z", "D", 0, 0, 1, 2), ("z", "D", 0, 1, 0, 2), ("z", "D", 0, 0, 0, 3), ("z", "C", 0, 0, 0, 2), ("1", "B", 0, 0, 3),
        ("z", "D", 0, 0, 0, 2), ("z", "C", 0, 1, 1, 0), ("z", "D", 0, 1, 1, 0), ("1", "A", 0, 0, 0), ("1", "A", 0, 1, 1),
        ("2", "A", 0, 0), ("z", "C", 0, 0, 1, 0), ("z", "C", 0, 1, 0, 0), ("z", "D", 0, 0, 1, 0), ("z", "D", 0, 1, 0, 0),
        ("3", "A", 0, 3), ("2", "A", 0, 2), ("z", "C", 0, 0, 0, 0), ("z", "D", 0, 0, 0, 0), ("1", "A", 0, 0, 2),
        ("2", "B", 0, 0), ("1", "B", 0, 0, 0), ("1", "B", 0, 1, 1), ("2", "B", 0, 2), ("x", "C", 0, 1), ("1", "B", 0, 0, 2),
        ("x", "D", 0, 1), ("1", "A", 0, 0, 1), ("x", "C", 0, 0), ("2", "A", 0, 1), ("3", "A", 0, 0), ("3", "B", 0, 3),
        ("1", "B", 0, 0, 1), ("2", "B", 0, 1), ("3", "B", 0, 0), ("3", "A", 0, 2), ("y", "C", 0), ("y", "D", 0),
        ("x", "D", 0, 0), ("3", "B", 0, 2),
    ),
    (
        ("1", "A", 0, 1, 0), ("1", "B", 0, 1, 0), ("1", "A", 0, 1, 1), ("1", "A", 0, 1, 3), ("1", "B", 0, 1, 1),
        ("1", "B", 0, 1, 3), ("z", "C", 0, 1, 1, 3), ("z", "C", 0, 1, 1, 0), ("z", "D", 0, 1, 1, 3), ("z", "D", 0, 1, 1, 0),
        ("z", "C", 0, 1, 1, 1), ("z", "D", 0, 1, 1, 1), ("1", "A", 0, 0, 0), ("2", "B", 0, 0), ("2", "A", 0, 0),
        ("z", "C", 0, 0, 1, 3), ("z", "C", 0, 0, 1, 0), ("z", "C", 0, 1, 0, 3), ("z", "C", 0, 1, 0, 0), ("z", "D", 0, 0, 1, 3),
        ("z", "D", 0, 0, 1, 0), ("z", "D", 0, 1, 0, 3), ("z", "D", 0, 1, 0, 0), ("z", "C", 0, 0, 1, 1), ("z", "C", 0, 1, 0, 1),
        ("1", "B", 0, 0, 0), ("z", "D", 0, 0, 1, 1), ("z", "C", 0, 0, 0, 3), ("z", "C", 0, 0, 0, 0), ("z", "D", 0, 0, 0, 0),
        ("z", "D", 0, 1, 0, 1), ("z", "D", 0, 0, 0, 3), ("z", "C", 0, 0, 0, 1), ("1", "A", 0, 0, 1), ("1", "A", 0, 1, 2),
        ("2", "A", 0, 1), ("z", "D", 0, 0, 0, 1), ("3", "A", 0, 0), ("2", "A", 0, 3), ("3", "B", 0, 0), ("1", "A", 0, 0, 3),
        ("2", "B", 0, 1), ("1", "B", 0, 0, 1), ("1", "B", 0, 1, 2), ("2", "B", 0, 3), ("x", "C", 0, 1), ("1", "B", 0, 0, 3),
        ("3", "A", 0, 3), ("x", "D", 0, 1), ("1", "A", 0, 0, 2), ("x", "C", 0, 0), ("2", "A", 0, 2), ("1", "B", 0, 0, 2),
        ("2", "B", 0, 2), ("3", "A", 0, 1), ("3", "B", 0, 3), ("y", "C", 0), ("y", "D", 0), ("x", "D", 0, 0), ("3", "B", 0, 1),
    ),
    (
        ("1", "A", 0, 1, 0), ("1", "B", 0, 1, 0), ("z", "C", 0, 1, 1, 0), ("z", "D", 0, 1, 1, 0), ("z", "C", 0, 1, 1, 1),
        ("z", "D", 0, 1, 1, 1), ("z", "C", 0, 1, 1, 2), ("z", "C", 0, 0, 1, 0), ("z", "C", 0, 1, 0, 0), ("1", "A", 0, 1, 1),
        ("1", "A", 0, 1, 2), ("1", "B", 0, 1, 1), ("z", "D", 0, 0, 1, 0), ("z", "D", 0, 1, 0, 0), ("z", "C", 0, 0, 1, 1),
        ("z", "C", 0, 1, 0, 1), ("z", "D", 0, 0, 1, 1), ("z", "C", 0, 0, 0, 0), ("z", "D", 0, 0, 0, 0), ("1", "B", 0, 1, 2),
        ("1", "B", 0, 0, 0), ("z", "D", 0, 1, 0, 1), ("z", "D", 0, 1, 1, 2), ("z", "C", 0, 0, 0, 1), ("z", "C", 0, 0, 1, 2),
        ("z", "C", 0, 1, 0, 2), ("z", "D", 0, 0, 0, 1), ("z", "D", 0, 0, 1, 2), ("1", "A", 0, 0, 0), ("2", "B", 0, 0),
        ("z", "D", 0, 1, 0, 2), ("z", "C", 0, 0, 0, 2), ("z", "D", 0, 0, 0, 2), ("2", "A", 0, 0), ("1", "A", 0, 0, 1),
        ("2", "B", 0, 1), ("2", "A", 0, 1), ("1", "B", 0, 0, 1), ("3", "B", 0, 0), ("1", "A", 0, 0, 2), ("1", "A", 0, 1, 3),
        ("2", "A", 0, 2), ("3", "A", 0, 0), ("1", "B", 0, 0, 2), ("3", "A", 0, 1), ("2", "B", 0, 2), ("x", "C", 0, 1),
        ("1", "B", 0, 1, 3), ("3", "B", 0, 1), ("x", "D", 0, 1), ("3", "A", 0, 2), ("1", "A", 0, 0, 3), ("x", "C", 0, 0),
        ("1", "B", 0, 0, 3), ("2", "A", 0, 3), ("3", "B", 0, 2), ("2", "B", 0, 3), ("y", "C", 0), ("y", "D", 0),
        ("x", "D", 0, 0),
    ),
)


def adamw_shard(grad, weight_now, moment_now, second_now):
    new_m = 0.9 * moment_now + 0.1 * grad
    new_v = 0.95 * second_now + 0.05 * grad * grad
    corr_m = new_m / (1.0 - 0.9**10)
    corr_v = new_v / (1.0 - 0.95**10)
    new_w = weight_now - 0.01 * (corr_m / (jnp.sqrt(corr_v) + 1e-08) + 0.1 * weight_now)
    return (new_w, new_m, new_v)


def adamw_kernel(grad, weight, moment, second, new_weight, new_moment, new_second):
    new_w, new_m, new_v = adamw_shard(grad[...], weight[...], moment[...], second[...])
    new_weight[...] = new_w
    new_moment[...] = new_m
    new_second[...] = new_v


def dp_digits(mesh):
    size = mesh.shape["dp"]
    line = mesh.devices.reshape(size, -1)[:, 0]
    digits = []
    if hasattr(line[0], "coords"):
        for axis in range(3):
            at = [device.coords[axis] for device in line]
            if len(set(at)) > 1:
                digits.append((len(set(at)), next(j for j in range(size) if at[j] != at[0])))
    total = 1
    for count, stride in digits:
        total *= count
    if total != size:
        digits = [(size, 1)] if size > 1 else []
    digits.sort()
    return [(1, 1)] * (3 - len(digits)) + digits


def axis_orders(digits):
    a, b, c = digits
    return [(a, b, c), (b, a, c), (c, a, b), (c, b, a)]


def row_spans(shard_rows):
    late = shard_rows // 128 * 8
    early = (shard_rows - 2 * late) // 2
    spans = [(0, early), (early, early), (2 * early, late), (2 * early + late, late)]
    return spans[:4 if late else 2]


def reduce_kernel(digits, micro, pieces, acts, cotan, counts, out, acts_held, cotan_held, acts_out, cotan_out, acts_in, cotan_in, rhs,
                  grad, got1, got2, got3, load_sem, part_send, part_recv, send1, recv1, send2, recv2, send3, recv3):
    sections = lax.axis_size("section")
    section = lax.axis_index("section")
    dp = lax.axis_index("dp")
    mirror = sections - 1 - section

    def moved(step, digit):
        count, stride = digit
        mine = lax.rem(lax.div(dp, stride), count)
        return (lax.rem(mine + step, count) - mine) * stride

    peers = [(dp, mirror)]
    for digit in digits:
        peers += [(dp + moved(step, digit), section) for step in range(1, digit[0])]
    barrier = pltpu.get_barrier_semaphore()
    for peer in peers:
        pl.semaphore_signal(barrier, inc=1, device_id=peer, device_id_type=MESH)
    loads = [
        pltpu.make_async_copy(cotan, cotan_held, load_sem.at[0]),
        pltpu.make_async_copy(acts.at[1], acts_held.at[1], load_sem.at[1]),
        pltpu.make_async_copy(acts.at[0], acts_held.at[0], load_sem.at[2]),
    ]
    for load in loads:
        load.start()

    rows, depth = acts.shape[1], acts.shape[2]
    width = cotan.shape[2]
    slots = rows // micro
    shard_rows = out.shape[0]
    orders = axis_orders(digits)
    spans = row_spans(shard_rows)
    last = digits[2]
    per_row = width // LANES

    def masked(k):
        parts = []
        for b in range(micro):
            block = cotan_held[k, b * slots:(b + 1) * slots, :].astype(jnp.float32)
            place = lax.broadcasted_iota(jnp.int32, (slots, width), 0)
            parts.append(jnp.where(place < counts[b, k], block, 0.0))
        return parts[0] if micro == 1 else jnp.concatenate(parts, axis=0)

    steps3 = sorted(range(1, last[0]), key=lambda step: -min(step, last[0] - step)) + [0]
    piece = depth // pieces
    by_owner = pieces == lax.axis_size("dp")
    kinds = {"forward": [], "own": [], "mine": []}
    for step_a in range(digits[0][0]):
        for step_b in range(digits[1][0]):
            kind = "forward" if step_a and step_b else "own" if step_a or step_b else "mine"
            kinds[kind].append((step_a, step_b))
    groups = [("forward", 0), ("own", 0), ("forward", 1)]
    groups += [(kind, i) for i in range(len(steps3)) for kind in ("own", "forward", "mine") if (kind, i) not in groups]
    owners, places, group_of = [], [], {}
    for kind, i in groups:
        if i < len(steps3):
            group_of[kind, i] = range(len(owners), len(owners) + len(kinds[kind]))
            for step_a, step_b in kinds[kind]:
                places.append((step_a, step_b, steps3[i]))
                owners.append(dp + moved(step_a, digits[0]) + moved(step_b, digits[1]) + moved(steps3[i], last))
    if not by_owner:
        owners = list(range(pieces))

    def columns(at):
        start = owners[at] * piece
        return pl.ds(start if isinstance(start, int) else pl.multiple_of(start, LANES), piece)

    def to_mirror(src, dst, at):
        return pltpu.make_async_remote_copy(
            src_ref=src, dst_ref=dst, send_sem=part_send.at[at], recv_sem=part_recv.at[at],
            device_id=(dp, mirror), device_id_type=MESH)

    exchange = [to_mirror(acts_out.at[at], acts_in.at[at], at) for at in range(pieces)]
    exchange.append(to_mirror(cotan_out, cotan_in, pieces))
    loads[0].wait()
    cotan_out[...] = masked(1)
    rhs[0:rows, :] = masked(0).astype(jnp.bfloat16)
    loads[1].wait()
    for at in range(pieces):
        acts_out[at] = acts_held[1, :, columns(at)].astype(jnp.float32)
    pl.semaphore_wait(barrier, len(peers))
    exchange[pieces].start()
    for copy in exchange[:pieces]:
        copy.start()
    loads[2].wait()
    exchange[pieces].wait_recv()
    rhs[rows:2 * rows, :] = cotan_in[...].astype(jnp.bfloat16)

    def make(at):
        exchange[at].wait_recv()
        lhs = jnp.concatenate([acts_held[0, :, columns(at)], acts_in[at].astype(jnp.bfloat16)], axis=0)
        product = lax.dot_general(lhs, rhs[...], (((0,), (0,)), ((), ())), preferred_element_type=jnp.float32)
        first = owners[at] * (piece * per_row)
        if not isinstance(first, int):
            first = pl.multiple_of(first, 8)
        for c in range(per_row):
            grad[pl.ds(first + c, piece, stride=per_row), :] = product[:, c * LANES:(c + 1) * LANES]

    def make_group(kind, i):
        if by_owner and (kind, i) in group_of:
            for at in group_of.pop((kind, i)):
                make(at)
                made.append(places[at])

    made = []
    if not by_owner:
        for at in range(pieces):
            make(at)
        made += places

    def block(o, step1, step2, step3):
        first, second, third = orders[o]
        owner = dp + moved(step1, first) + moved(step2, second) + moved(step3, third)
        return grad.at[pl.ds(pl.multiple_of(owner * shard_rows + spans[o][0], 8), spans[o][1]), :]

    def base1(o, step1, step2, step3):
        first, second, third = orders[o]
        return ((step1 - 1) * second[0] + step2) * third[0] + step3

    def stage1(o, step1, step2, step3):
        at = base1(o, step1, step2, step3)
        return pltpu.make_async_remote_copy(
            src_ref=block(o, step1, step2, step3), dst_ref=got1[o].at[at], send_sem=send1[o].at[at], recv_sem=recv1[o].at[at],
            device_id=(dp + moved(step1, orders[o][0]), section), device_id_type=MESH)

    def stage2(o, step2, step3):
        at = (step2 - 1) * orders[o][2][0] + step3
        return pltpu.make_async_remote_copy(
            src_ref=block(o, 0, step2, step3), dst_ref=got2[o].at[at], send_sem=send2[o].at[at], recv_sem=recv2[o].at[at],
            device_id=(dp + moved(step2, orders[o][1]), section), device_id_type=MESH)

    def stage3(o, step3):
        at = step3 - 1
        return pltpu.make_async_remote_copy(
            src_ref=block(o, 0, 0, step3), dst_ref=got3[o].at[at], send_sem=send3[o].at[at], recv_sem=recv3[o].at[at],
            device_id=(dp + moved(step3, orders[o][2]), section), device_id_type=MESH)

    started = []

    def start(copy):
        copy.start()
        started.append(copy)

    def arrived1(o, step2, step3):
        total = block(o, 0, step2, step3)[...]
        for step1 in range(1, orders[o][0][0]):
            stage1(o, step1, step2, step3).wait_recv()
            total += got1[o][base1(o, step1, step2, step3)]
        return total

    def arrived2(o, step3):
        total = arrived1(o, 0, step3)
        for step2 in range(1, orders[o][1][0]):
            stage2(o, step2, step3).wait_recv()
            total += got2[o][(step2 - 1) * orders[o][2][0] + step3]
        return total

    def send_forward(i):
        if i < len(steps3):
            for o in range(2):
                for step1 in range(1, orders[o][0][0]):
                    for step2 in range(1, orders[o][1][0]):
                        start(stage1(o, step1, step2, steps3[i]))

    def send_own(i):
        if i < len(steps3):
            for o in range(2):
                for step1 in range(1, orders[o][0][0]):
                    start(stage1(o, step1, 0, steps3[i]))

    def send_second(i):
        for o in range(2):
            for step2 in range(1, orders[o][1][0]):
                block(o, 0, step2, steps3[i])[...] = arrived1(o, step2, steps3[i])
                start(stage2(o, step2, steps3[i]))

    def send_third(i):
        for o in range(2):
            block(o, 0, 0, steps3[i])[...] = arrived2(o, steps3[i])
            start(stage3(o, steps3[i]))

    late = range(2, len(spans))

    def late_first(step2, step3, step1):
        for o in late:
            if step1:
                start(stage1(o, step1, *((step2, step3) if orders[o][1] is digits[0] else (step3, step2))))

    def late_second():
        for o in late:
            for step2 in range(1, orders[o][1][0]):
                for step3 in reversed(range(orders[o][2][0])):
                    block(o, 0, step2, step3)[...] = arrived1(o, step2, step3)
                    start(stage2(o, step2, step3))

    def late_third():
        for o in late:
            for step3 in range(1, orders[o][2][0]):
                block(o, 0, 0, step3)[...] = arrived2(o, step3)
                start(stage3(o, step3))

    def send_late():
        while made:
            late_first(*made.pop(0))

    end = len(steps3) - 1
    make_group("forward", 0)
    send_forward(0)
    make_group("own", 0)
    send_own(0)
    send_late()
    make_group("forward", 1)
    if end > 1:
        send_forward(1)
    send_late()
    for kind, i in list(group_of):
        make_group(kind, i)
        send_late()
    for i in range(end + 1):
        if i == end and i:
            send_third(i - 1)
        send_second(i)
        if i == end - 1:
            send_forward(end)
        send_own(i + 1)
        if i + 2 < end:
            send_forward(i + 2)
        if 1 <= i < end:
            send_third(i - 1)
        if i == end - 2:
            late_second()
        if i == end - 1:
            late_third()
    if len(steps3) < 3:
        late_second()
    if len(steps3) < 2:
        late_third()
    for o in reversed(range(len(spans))):
        total = arrived2(o, 0)
        for step3 in range(1, orders[o][2][0]):
            stage3(o, step3).wait_recv()
            total += got3[o][step3 - 1]
        out[spans[o][0]:spans[o][0] + spans[o][1], :] = total
    for copy in exchange + started:
        copy.wait_send()


def shards(digits, acts, cotan, counts, weight, moment, second):
    micro = counts.shape[3]
    rows, depth = acts.shape[2], acts.shape[3]
    width = cotan.shape[3]
    shard_rows = weight.shape[1] // LANES
    piece = weight.shape[1] // width
    pieces = depth // piece if piece % LANES == 0 and weight.shape[1] % width == 0 else depth // (2 * LANES)
    orders = axis_orders(digits)
    spans = row_spans(shard_rows)
    orders = orders[:len(spans)]
    counts1 = [(first[0] - 1) * second[0] * third[0] for first, second, third in orders]
    counts2 = [(second[0] - 1) * third[0] for first, second, third in orders]
    counts3 = [third[0] - 1 for first, second, third in orders]

    def buffers(sizes):
        return [pltpu.VMEM((max(size, 1), span[1], LANES), jnp.float32) for size, span in zip(sizes, spans)]

    def semaphores(sizes):
        return [pltpu.SemaphoreType.DMA((max(size, 1),)) for size in sizes]

    hbm = pl.BlockSpec(memory_space=pl.ANY)
    vmem = pl.BlockSpec(memory_space=pltpu.VMEM)
    shard = pl.pallas_call(
        functools.partial(reduce_kernel, digits, micro, pieces),
        out_shape=jax.ShapeDtypeStruct((shard_rows, LANES), jnp.float32),
        in_specs=[hbm, hbm, pl.BlockSpec(memory_space=pltpu.SMEM)],
        out_specs=vmem,
        scratch_shapes=[
            pltpu.VMEM((2, rows, depth), jnp.bfloat16),
            pltpu.VMEM((2, rows, width), jnp.bfloat16),
            pltpu.VMEM((pieces, rows, depth // pieces), jnp.float32),
            pltpu.VMEM((rows, width), jnp.float32),
            pltpu.VMEM((pieces, rows, depth // pieces), jnp.float32),
            pltpu.VMEM((rows, width), jnp.float32),
            pltpu.VMEM((2 * rows, width), jnp.bfloat16),
            pltpu.VMEM((depth * width // LANES, LANES), jnp.float32),
            buffers(counts1), buffers(counts2), buffers(counts3),
            pltpu.SemaphoreType.DMA((3,)), pltpu.SemaphoreType.DMA((pieces + 1,)), pltpu.SemaphoreType.DMA((pieces + 1,)),
            semaphores(counts1), semaphores(counts1), semaphores(counts2), semaphores(counts2),
            semaphores(counts3), semaphores(counts3),
        ],
        compiler_params=pltpu.CompilerParams(collective_id=0, has_side_effects=True),
        name="reduce_grad",
    )(acts[0], cotan[0], counts[0, :, 0, :].T)
    flat = jax.ShapeDtypeStruct((shard_rows, LANES), jnp.float32)
    outs = pl.pallas_call(
        adamw_kernel,
        out_shape=(flat, flat, flat),
        in_specs=[vmem] * 4,
        out_specs=(vmem, vmem, vmem),
        name="adamw",
    )(shard, *(array.reshape(shard_rows, LANES) for array in (weight, moment, second)))
    return tuple(array.reshape(weight.shape) for array in outs)


AXES = {"A": (0, 1), "B": (1, 0), "C": (0, 1), "D": (1, 0)}


def flipped(family, first, second):
    return (first, second) if AXES[family][0] == 0 else (second, first)


def planes_beside(z, planes):
    return [p for p in (z - 1, z + 1) if 0 <= p < planes]


def send_table(z, planes):
    table = {}
    for f, chunks in CHUNKS.items():
        first, second = AXES[f]
        for k in range(planes):
            for c in range(len(chunks)):
                if f in "AB":
                    for b in range(2):
                        table["1", f, c, b, k] = (first, z, (), flipped(f, 1, b) + (k,))
                    table["2", f, c, k] = (second, z, (("1", f, c, 1, k),), flipped(f, 0, 1) + (k,))
                    if k != z:
                        table["3", f, c, k] = (2, k, (("1", f, c, 0, k), ("2", f, c, k)), (0, 0, k))
                elif k != z:
                    toward = 1 if k > z else -1
                    for a in range(2):
                        for b in range(2):
                            before = z - toward
                            needs = (("z", f, c, a, b, k, before),) if 0 <= before < planes else ()
                            table["z", f, c, a, b, k] = (2, z + toward, needs, (a, b, k))
                else:
                    def crossed(place):
                        return tuple(("z", f, c, *place, z, p) for p in planes_beside(z, planes))

                    for b in range(2):
                        place = flipped(f, 1, b)
                        table["x", f, c, b] = (first, z, crossed(place), place + (z,))
                    place = flipped(f, 0, 1)
                    table["y", f, c] = (second, z, crossed(place) + (("x", f, c, 1),), place + (z,))
    return table


def last_needs(f, c, z, planes):
    if f in "AB":
        return [("1", f, c, 0, z), ("2", f, c, z)] + [("3", f, c, p) for p in range(planes) if p != z]
    return [("z", f, c, 0, 0, z, p) for p in planes_beside(z, planes)] + [("x", f, c, 0), ("y", f, c)]


def key_there(key, z):
    return key[:-1] + (z,) if key[0] == "3" else key + (z,) if key[0] == "z" else key


def spans_of(piece):
    tiles = piece // 8
    total = sum(sum(chunks) for chunks in CHUNKS.values())
    spans, at = {}, 0
    for f, chunks in CHUNKS.items():
        for c, size in enumerate(chunks):
            rows = size * tiles // total * 8
            spans[f, c] = (at, rows)
            at += rows
    return spans


def arrivals(z, planes, spans):
    slots, at = {}, 0
    for source in range(planes):
        for key, (axis, target, needs, owner) in send_table(source, planes).items():
            if target == z:
                rows = spans[key[1], key[2]][1]
                slots[key_there(key, source)] = (at, rows, len(slots))
                at += rows
    return slots, at


def fast_kernel(digits, micro, acts, cotan, counts, weight, moment, second, packed, counts_held, acts_held, cotan_held,
                acts_out, cotan_out, acts_in, cotan_in, rhs, grad, got, state, shard, load_sem, part_send, part_recv,
                send_sem, recv_sem, up_sem):
    section = lax.axis_index("section")
    dp = lax.axis_index("dp")
    mirror = (dp, lax.axis_size("section") - 1 - section)
    planes = digits[2][0]
    strides = [stride for count, stride in digits]
    here = [lax.rem(lax.div(dp, stride), count) for count, stride in digits]
    across = [(1 - 2 * here[axis]) * strides[axis] for axis in range(2)]
    rows, depth = acts.shape[1], acts.shape[2]
    width = cotan.shape[2]
    slots = rows // micro
    pieces = lax.axis_size("dp")
    piece = depth // pieces
    per_row = width // LANES
    spans = spans_of(piece)
    tables = [send_table(z, planes) for z in range(planes)]
    landings = [arrivals(z, planes, spans)[0] for z in range(planes)]

    loads = [
        pltpu.make_async_copy(cotan, cotan_held, load_sem.at[0]),
        pltpu.make_async_copy(counts, counts_held, load_sem.at[1]),
        pltpu.make_async_copy(acts.at[1], acts_held.at[1], load_sem.at[2]),
        pltpu.make_async_copy(acts.at[0], acts_held.at[0], load_sem.at[3]),
    ]
    loads += [pltpu.make_async_copy(array, state.at[i], load_sem.at[4 + i]) for i, array in enumerate((weight, moment, second))]
    for load in loads[:4]:
        load.start()

    barrier = pltpu.get_barrier_semaphore()
    pl.semaphore_signal(barrier, inc=1, device_id=mirror, device_id_type=MESH)
    for axis in range(2):
        @pl.when(here[axis] == 0)
        def greet():
            pl.semaphore_signal(barrier, inc=1, device_id=(dp + across[axis], section), device_id_type=MESH)
    for step in range(1, planes):
        @pl.when(here[2] + step < planes)
        def greet_plane():
            pl.semaphore_signal(barrier, inc=1, device_id=(dp + step * strides[2], section), device_id_type=MESH)

    def masked(k):
        parts = []
        for b in range(micro):
            block = cotan_held[k, b * slots:(b + 1) * slots, :].astype(jnp.float32)
            place = lax.broadcasted_iota(jnp.int32, (slots, width), 0)
            parts.append(jnp.where(place < counts_held[b, k], block, 0.0))
        return parts[0] if micro == 1 else jnp.concatenate(parts, axis=0)

    def to_mirror(src, dst, at):
        return pltpu.make_async_remote_copy(
            src_ref=src, dst_ref=dst, send_sem=part_send.at[at], recv_sem=part_recv.at[at],
            device_id=mirror, device_id_type=MESH)

    exchange = [to_mirror(acts_out.at[at], acts_in.at[at], at) for at in range(pieces)]
    exchange.append(to_mirror(cotan_out, cotan_in, pieces))
    loads[0].wait()
    loads[1].wait()
    cotan_out[...] = masked(1)
    pl.semaphore_wait(barrier, 1 + here[0] + here[1] + here[2])
    exchange[pieces].start()
    rhs[0:rows, :] = masked(0).astype(jnp.bfloat16)
    for axis in range(2):
        @pl.when(here[axis] == 1)
        def answer():
            pl.semaphore_signal(up_sem.at[axis], inc=1, device_id=(dp + across[axis], section), device_id_type=MESH)
    for step in range(1, planes):
        @pl.when(here[2] >= step)
        def answer_plane():
            pl.semaphore_signal(up_sem.at[1 + step], inc=1, device_id=(dp - step * strides[2], section), device_id_type=MESH)
    loads[2].wait()

    def run(z):
        table, landing = tables[z], landings[z]
        order = ORDERS[z]
        owners = []
        for key in order:
            if table[key][3] not in owners:
                owners.append(table[key][3])
        owners.append((0, 0, z))

        def owner_index(owner):
            return dp + owner[0] * across[0] + owner[1] * across[1] + (owner[2] - z) * strides[2]

        def columns(owner):
            return pl.ds(pl.multiple_of(owner_index(owner) * piece, LANES), piece)

        for at, owner in enumerate(owners):
            acts_out[at] = acts_held[1, :, columns(owner)].astype(jnp.float32)
            exchange[at].start()
        for load in loads[4:]:
            load.start()
        loads[3].wait()
        exchange[pieces].wait_recv()
        rhs[rows:2 * rows, :] = cotan_in[...].astype(jnp.bfloat16)

        def make(at):
            exchange[at].wait_recv()
            lhs = jnp.concatenate([acts_held[0, :, columns(owners[at])], acts_in[at].astype(jnp.bfloat16)], axis=0)
            first = pl.multiple_of(owner_index(owners[at]) * piece, piece)
            grad[pl.ds(first, piece), :] = lax.dot_general(
                lhs, rhs[...], (((0,), (0,)), ((), ())), preferred_element_type=jnp.float32)

        def block(owner, span):
            return pl.ds(pl.multiple_of(owner_index(owner) * piece + span[0], 8), span[1])

        def copy_of(key):
            axis, target, needs, owner = table[key]
            place, size, at = landings[target][key_there(key, z)]
            device = dp + across[axis] if axis < 2 else dp + (target - z) * strides[2]
            return pltpu.make_async_remote_copy(
                src_ref=grad.at[block(owner, spans[key[1], key[2]]), :], dst_ref=got.at[pl.ds(place, size), :],
                send_sem=send_sem.at[sends.index(key)], recv_sem=recv_sem.at[at],
                device_id=(device, section), device_id_type=MESH)

        def arrived(key):
            place, size, at = landing[key]
            pltpu.make_async_remote_copy(
                src_ref=grad.at[pl.ds(0, size), :], dst_ref=got.at[pl.ds(place, size), :],
                send_sem=send_sem.at[0], recv_sem=recv_sem.at[at],
                device_id=mirror, device_id_type=MESH).wait_recv()
            return got[place:place + size, :]

        sends = list(order)
        met, done = set(), 0
        for key in order:
            axis, target, needs, owner = table[key]
            while done <= owners.index(owner):
                make(done)
                done += 1
            if needs:
                at = block(owner, spans[key[1], key[2]])
                total = grad[at, :]
                for need in needs:
                    total += arrived(need)
                grad[at, :] = total
            if axis < 2 and axis not in met:
                met.add(axis)

                @pl.when(here[axis] == 0)
                def wait_up():
                    pl.semaphore_wait(up_sem.at[axis], 1)
            if axis == 2 and target > z and 1 + target - z not in met:
                met.add(1 + target - z)
                pl.semaphore_wait(up_sem.at[1 + target - z], 1)
            copy_of(key).start()
        while done < pieces:
            make(done)
            done += 1
        for load in loads[4:]:
            load.wait()
        for f, c in FINALS:
            span = spans[f, c]
            total = grad[block((0, 0, z), span), :]
            for need in last_needs(f, c, z, planes):
                total += arrived(need)
            for part in range(per_row):
                shard[pl.ds(span[0] * per_row + part, span[1], stride=per_row), :] = total[:, part * LANES:(part + 1) * LANES]
            flat = slice(span[0] * per_row, (span[0] + span[1]) * per_row)
            updated = adamw_shard(shard[flat, :], state[0, flat, :], state[1, flat, :], state[2, flat, :])
            for i in range(3):
                packed[i, flat, :] = updated[i]
        for copy in exchange:
            copy.wait_send()
        for key in sends:
            copy_of(key).wait_send()

    for z in range(planes):
        pl.when(here[2] == z)(functools.partial(run, z))


def put_kernel(packed, new_weight, new_moment, new_second, sem):
    copies = [pltpu.make_async_copy(packed.at[i], out, sem.at[i]) for i, out in enumerate((new_weight, new_moment, new_second))]
    for copy in copies:
        copy.start()
    for copy in copies:
        copy.wait()


def fast_fits(digits, acts, cotan, weight):
    planes, depth, width = digits[2][0], acts.shape[3], cotan.shape[3]
    piece = depth // (4 * planes)
    total = sum(sum(chunks) for chunks in CHUNKS.values())
    return (digits[0][0] == 2 and digits[1][0] == 2 and planes == len(ORDERS) and piece % LANES == 0 and piece % (8 * total) == 0
            and width % LANES == 0 and piece * width == weight.shape[1])


def fast_shards(digits, acts, cotan, counts, weight, moment, second):
    micro = counts.shape[3]
    rows, depth = acts.shape[2], acts.shape[3]
    width = cotan.shape[3]
    shard_rows = weight.shape[1] // LANES
    planes = digits[2][0]
    pieces = 4 * planes
    spans = spans_of(depth // pieces)
    landings = [arrivals(z, planes, spans) for z in range(planes)]
    received = max(len(slots) for slots, total in landings)
    space = max(total for slots, total in landings)
    sent = max(len(send_table(z, planes)) for z in range(planes))
    hbm = pl.BlockSpec(memory_space=pl.ANY)
    vmem = pl.BlockSpec(memory_space=pltpu.VMEM)
    flat = (shard_rows, LANES)
    packed = pl.pallas_call(
        functools.partial(fast_kernel, digits, micro),
        out_shape=pltpu.VMEM((3, *flat), jnp.float32),
        in_specs=[hbm] * 6,
        out_specs=vmem,
        scratch_shapes=[
            pltpu.SMEM((micro, 2), jnp.int32),
            pltpu.VMEM((2, rows, depth), jnp.bfloat16),
            pltpu.VMEM((2, rows, width), jnp.bfloat16),
            pltpu.VMEM((pieces, rows, depth // pieces), jnp.float32),
            pltpu.VMEM((rows, width), jnp.float32),
            pltpu.VMEM((pieces, rows, depth // pieces), jnp.float32),
            pltpu.VMEM((rows, width), jnp.float32),
            pltpu.VMEM((2 * rows, width), jnp.bfloat16),
            pltpu.VMEM((depth, width), jnp.float32),
            pltpu.VMEM((space, width), jnp.float32),
            pltpu.VMEM((3, *flat), jnp.float32),
            pltpu.VMEM(flat, jnp.float32),
            pltpu.SemaphoreType.DMA((7,)), pltpu.SemaphoreType.DMA((pieces + 1,)), pltpu.SemaphoreType.DMA((pieces + 1,)),
            pltpu.SemaphoreType.DMA((sent,)), pltpu.SemaphoreType.DMA((received,)),
            pltpu.SemaphoreType.REGULAR((1 + planes,)),
        ],
        compiler_params=pltpu.CompilerParams(collective_id=0, has_side_effects=True, vmem_limit_bytes=66 * 10**6),
        name="reduce_adamw",
    )(acts[0], cotan[0], counts[0, :, 0, :].T, *(array.reshape(flat) for array in (weight, moment, second)))
    outs = pl.pallas_call(
        put_kernel,
        out_shape=(jax.ShapeDtypeStruct(flat, jnp.float32),) * 3,
        in_specs=[vmem],
        out_specs=(hbm, hbm, hbm),
        scratch_shapes=[pltpu.SemaphoreType.DMA((3,))],
        name="put",
    )(pltpu.with_memory_space_constraint(packed, pltpu.VMEM))
    return tuple(array.reshape(weight.shape) for array in outs)


def solution(mesh):
    in_specs = (
        P("section", None, "dp", None),
        P("section", None, "dp", None),
        P("section", None, "dp", None),
        P("section", "dp"),
        P("section", "dp"),
        P("section", "dp"),
    )
    out_specs = (P("section", "dp"), P("section", "dp"), P("section", "dp"))
    digits = dp_digits(mesh)

    def body(acts, cotan, counts, weight, moment, second):
        form = fast_shards if fast_fits(digits, acts, cotan, weight) else shards
        return form(digits, acts, cotan, counts, weight, moment, second)

    return jax.shard_map(body, mesh=mesh, in_specs=in_specs, out_specs=out_specs, check_vma=False)
```

```python
import functools
import jax
import jax.numpy as jnp
from jax import lax
from jax.experimental import pallas as pl
from jax.experimental.pallas import tpu as pltpu
from jax.sharding import PartitionSpec as P

LANES = 128
MESH = pl.DeviceIdType.MESH


CHUNKS = {"A": (7,), "B": (6,), "Z": ((1, 2),)}
LASTS = (
    (("C", 0), ("D", 0), ("A", 0), ("B", 0)),
    (("C", 0), ("D", 0), ("A", 0), ("B", 0)),
    (("C", 0), ("D", 0), ("A", 0), ("B", 0)),
    (("C", 0), ("D", 0), ("A", 0), ("B", 0)),
)
ORDERS = (
    (
        ("1", "A", 0, 1, 2), ("z", 0, 0, 1, 3), ("1", "B", 0, 1, 1), ("z", 0, 1, 0, 3), ("z", 0, 1, 1, 3), ("z", 0, 0, 0, 3),
        ("1", "A", 0, 1, 3), ("z", 0, 1, 1, 2), ("z", 0, 1, 0, 2), ("1", "B", 0, 1, 0), ("z", 0, 0, 0, 2), ("1", "A", 0, 0, 3),
        ("z", 0, 1, 1, 1), ("2", "A", 0, 2), ("1", "A", 0, 1, 0), ("1", "A", 0, 1, 1), ("z", 0, 0, 1, 2), ("2", "A", 0, 3),
        ("1", "B", 0, 1, 3), ("z", 0, 0, 1, 1), ("1", "B", 0, 1, 2), ("z", 0, 1, 0, 1), ("1", "B", 0, 0, 3), ("z", 0, 0, 0, 1),
        ("1", "A", 0, 0, 2), ("1", "B", 0, 0, 1), ("2", "B", 0, 1), ("3", "A", 0, 3), ("2", "B", 0, 3), ("x", "D", 0, 1),
        ("1", "B", 0, 0, 2), ("x", "C", 0, 1), ("2", "B", 0, 2), ("1", "A", 0, 0, 1), ("2", "A", 0, 1), ("3", "A", 0, 2),
        ("2", "B", 0, 0), ("2", "A", 0, 0), ("3", "B", 0, 3), ("1", "A", 0, 0, 0), ("3", "B", 0, 1), ("y", "D", 0),
        ("1", "B", 0, 0, 0), ("x", "C", 0, 0), ("3", "B", 0, 2), ("3", "A", 0, 1), ("x", "D", 0, 0), ("y", "C", 0),
    ),
    (
        ("1", "A", 0, 1, 3), ("1", "B", 0, 1, 3), ("1", "A", 0, 1, 2), ("1", "B", 0, 1, 0), ("z", 0, 0, 1, 3),
        ("1", "A", 0, 1, 0), ("1", "B", 0, 1, 2), ("z", 0, 1, 1, 3), ("1", "A", 0, 0, 3), ("2", "A", 0, 3),
        ("1", "B", 0, 0, 1), ("z", 0, 1, 0, 3), ("1", "B", 0, 0, 3), ("z", 0, 1, 1, 2), ("1", "A", 0, 0, 2), ("z", 0, 0, 0, 3),
        ("2", "A", 0, 2), ("1", "B", 0, 1, 1), ("2", "B", 0, 3), ("z", 0, 1, 0, 2), ("2", "A", 0, 0), ("z", 0, 0, 0, 2),
        ("x", "C", 0, 1), ("z", 0, 1, 1, 0), ("z", 0, 0, 1, 2), ("z", 0, 0, 0, 0), ("1", "A", 0, 0, 0), ("3", "A", 0, 3),
        ("2", "B", 0, 2), ("z", 0, 0, 1, 0), ("x", "D", 0, 1), ("2", "B", 0, 0), ("3", "B", 0, 3), ("z", 0, 1, 0, 0),
        ("1", "A", 0, 0, 1), ("3", "A", 0, 2), ("1", "B", 0, 0, 0), ("1", "B", 0, 0, 2), ("3", "A", 0, 0), ("1", "A", 0, 1, 1),
        ("y", "C", 0), ("y", "D", 0), ("2", "B", 0, 1), ("x", "D", 0, 0), ("3", "B", 0, 0), ("3", "B", 0, 2), ("2", "A", 0, 1),
        ("x", "C", 0, 0),
    ),
    (
        ("1", "A", 0, 1, 0), ("1", "B", 0, 1, 0), ("1", "A", 0, 0, 0), ("1", "A", 0, 1, 1), ("1", "A", 0, 1, 3),
        ("1", "B", 0, 1, 1), ("1", "B", 0, 0, 0), ("z", 0, 1, 1, 1), ("2", "A", 0, 0), ("2", "B", 0, 0), ("z", 0, 1, 1, 0),
        ("1", "A", 0, 1, 2), ("z", 0, 0, 0, 0), ("z", 0, 0, 1, 3), ("z", 0, 0, 1, 1), ("1", "A", 0, 0, 3), ("z", 0, 0, 1, 0),
        ("1", "B", 0, 1, 3), ("z", 0, 1, 0, 0), ("1", "B", 0, 0, 1), ("z", 0, 1, 0, 3), ("z", 0, 1, 0, 1), ("2", "B", 0, 1),
        ("3", "A", 0, 0), ("1", "B", 0, 0, 3), ("x", "C", 0, 1), ("z", 0, 0, 0, 1), ("2", "A", 0, 3), ("z", 0, 0, 0, 3),
        ("x", "D", 0, 1), ("1", "A", 0, 0, 1), ("2", "A", 0, 1), ("2", "B", 0, 3), ("1", "B", 0, 1, 2), ("2", "A", 0, 2),
        ("z", 0, 1, 1, 3), ("3", "B", 0, 0), ("3", "A", 0, 3), ("x", "D", 0, 0), ("1", "A", 0, 0, 2), ("3", "B", 0, 1),
        ("x", "C", 0, 0), ("y", "D", 0), ("1", "B", 0, 0, 2), ("3", "B", 0, 3), ("3", "A", 0, 1), ("2", "B", 0, 2),
        ("y", "C", 0),
    ),
    (
        ("z", 0, 1, 1, 1), ("1", "A", 0, 1, 0), ("1", "B", 0, 1, 0), ("1", "A", 0, 0, 0), ("1", "A", 0, 1, 1),
        ("1", "B", 0, 1, 1), ("z", 0, 1, 1, 0), ("z", 0, 0, 0, 0), ("z", 0, 0, 1, 1), ("z", 0, 0, 1, 0), ("z", 0, 1, 0, 0),
        ("1", "B", 0, 1, 2), ("z", 0, 1, 0, 1), ("z", 0, 0, 0, 1), ("2", "B", 0, 0), ("1", "A", 0, 1, 2), ("z", 0, 1, 1, 2),
        ("1", "B", 0, 0, 0), ("1", "A", 0, 0, 1), ("2", "A", 0, 0), ("z", 0, 0, 1, 2), ("1", "B", 0, 0, 2), ("2", "A", 0, 1),
        ("2", "B", 0, 2), ("1", "B", 0, 0, 1), ("3", "B", 0, 0), ("1", "A", 0, 1, 3), ("z", 0, 0, 0, 2), ("1", "B", 0, 1, 3),
        ("3", "A", 0, 0), ("2", "B", 0, 1), ("1", "A", 0, 0, 2), ("2", "A", 0, 2), ("x", "D", 0, 0), ("z", 0, 1, 0, 2),
        ("3", "A", 0, 1), ("x", "D", 0, 1), ("1", "B", 0, 0, 3), ("x", "C", 0, 1), ("3", "B", 0, 2), ("x", "C", 0, 0),
        ("1", "A", 0, 0, 3), ("3", "B", 0, 1), ("2", "A", 0, 3), ("2", "B", 0, 3), ("3", "A", 0, 2), ("y", "D", 0),
        ("y", "C", 0),
    ),
)


def adamw_shard(grad, weight_now, moment_now, second_now):
    new_m = 0.9 * moment_now + 0.1 * grad
    new_v = 0.95 * second_now + 0.05 * grad * grad
    corr_m = new_m / (1.0 - 0.9**10)
    corr_v = new_v / (1.0 - 0.95**10)
    new_w = weight_now - 0.01 * (corr_m / (jnp.sqrt(corr_v) + 1e-08) + 0.1 * weight_now)
    return (new_w, new_m, new_v)


def adamw_kernel(grad, weight, moment, second, new_weight, new_moment, new_second):
    new_w, new_m, new_v = adamw_shard(grad[...], weight[...], moment[...], second[...])
    new_weight[...] = new_w
    new_moment[...] = new_m
    new_second[...] = new_v


def dp_digits(mesh):
    size = mesh.shape["dp"]
    line = mesh.devices.reshape(size, -1)[:, 0]
    digits = []
    if hasattr(line[0], "coords"):
        for axis in range(3):
            at = [device.coords[axis] for device in line]
            if len(set(at)) > 1:
                digits.append((len(set(at)), next(j for j in range(size) if at[j] != at[0])))
    total = 1
    for count, stride in digits:
        total *= count
    if total != size:
        digits = [(size, 1)] if size > 1 else []
    digits.sort()
    return [(1, 1)] * (3 - len(digits)) + digits


def axis_orders(digits):
    a, b, c = digits
    return [(a, b, c), (b, a, c), (c, a, b), (c, b, a)]


def row_spans(shard_rows):
    late = shard_rows // 128 * 8
    early = (shard_rows - 2 * late) // 2
    spans = [(0, early), (early, early), (2 * early, late), (2 * early + late, late)]
    return spans[:4 if late else 2]


def reduce_kernel(digits, micro, pieces, acts, cotan, counts, out, acts_held, cotan_held, acts_out, cotan_out, acts_in, cotan_in, rhs,
                  grad, got1, got2, got3, load_sem, part_send, part_recv, send1, recv1, send2, recv2, send3, recv3):
    sections = lax.axis_size("section")
    section = lax.axis_index("section")
    dp = lax.axis_index("dp")
    mirror = sections - 1 - section

    def moved(step, digit):
        count, stride = digit
        mine = lax.rem(lax.div(dp, stride), count)
        return (lax.rem(mine + step, count) - mine) * stride

    peers = [(dp, mirror)]
    for digit in digits:
        peers += [(dp + moved(step, digit), section) for step in range(1, digit[0])]
    barrier = pltpu.get_barrier_semaphore()
    for peer in peers:
        pl.semaphore_signal(barrier, inc=1, device_id=peer, device_id_type=MESH)
    loads = [
        pltpu.make_async_copy(cotan, cotan_held, load_sem.at[0]),
        pltpu.make_async_copy(acts.at[1], acts_held.at[1], load_sem.at[1]),
        pltpu.make_async_copy(acts.at[0], acts_held.at[0], load_sem.at[2]),
    ]
    for load in loads:
        load.start()

    rows, depth = acts.shape[1], acts.shape[2]
    width = cotan.shape[2]
    slots = rows // micro
    shard_rows = out.shape[0]
    orders = axis_orders(digits)
    spans = row_spans(shard_rows)
    last = digits[2]
    per_row = width // LANES

    def masked(k):
        parts = []
        for b in range(micro):
            block = cotan_held[k, b * slots:(b + 1) * slots, :].astype(jnp.float32)
            place = lax.broadcasted_iota(jnp.int32, (slots, width), 0)
            parts.append(jnp.where(place < counts[b, k], block, 0.0))
        return parts[0] if micro == 1 else jnp.concatenate(parts, axis=0)

    steps3 = sorted(range(1, last[0]), key=lambda step: -min(step, last[0] - step)) + [0]
    piece = depth // pieces
    by_owner = pieces == lax.axis_size("dp")
    kinds = {"forward": [], "own": [], "mine": []}
    for step_a in range(digits[0][0]):
        for step_b in range(digits[1][0]):
            kind = "forward" if step_a and step_b else "own" if step_a or step_b else "mine"
            kinds[kind].append((step_a, step_b))
    groups = [("forward", 0), ("own", 0), ("forward", 1)]
    groups += [(kind, i) for i in range(len(steps3)) for kind in ("own", "forward", "mine") if (kind, i) not in groups]
    owners, places, group_of = [], [], {}
    for kind, i in groups:
        if i < len(steps3):
            group_of[kind, i] = range(len(owners), len(owners) + len(kinds[kind]))
            for step_a, step_b in kinds[kind]:
                places.append((step_a, step_b, steps3[i]))
                owners.append(dp + moved(step_a, digits[0]) + moved(step_b, digits[1]) + moved(steps3[i], last))
    if not by_owner:
        owners = list(range(pieces))

    def columns(at):
        start = owners[at] * piece
        return pl.ds(start if isinstance(start, int) else pl.multiple_of(start, LANES), piece)

    def to_mirror(src, dst, at):
        return pltpu.make_async_remote_copy(
            src_ref=src, dst_ref=dst, send_sem=part_send.at[at], recv_sem=part_recv.at[at],
            device_id=(dp, mirror), device_id_type=MESH)

    exchange = [to_mirror(acts_out.at[at], acts_in.at[at], at) for at in range(pieces)]
    exchange.append(to_mirror(cotan_out, cotan_in, pieces))
    loads[0].wait()
    cotan_out[...] = masked(1)
    rhs[0:rows, :] = masked(0).astype(jnp.bfloat16)
    loads[1].wait()
    for at in range(pieces):
        acts_out[at] = acts_held[1, :, columns(at)].astype(jnp.float32)
    pl.semaphore_wait(barrier, len(peers))
    exchange[pieces].start()
    for copy in exchange[:pieces]:
        copy.start()
    loads[2].wait()
    exchange[pieces].wait_recv()
    rhs[rows:2 * rows, :] = cotan_in[...].astype(jnp.bfloat16)

    def make(at):
        exchange[at].wait_recv()
        lhs = jnp.concatenate([acts_held[0, :, columns(at)], acts_in[at].astype(jnp.bfloat16)], axis=0)
        product = lax.dot_general(lhs, rhs[...], (((0,), (0,)), ((), ())), preferred_element_type=jnp.float32)
        first = owners[at] * (piece * per_row)
        if not isinstance(first, int):
            first = pl.multiple_of(first, 8)
        for c in range(per_row):
            grad[pl.ds(first + c, piece, stride=per_row), :] = product[:, c * LANES:(c + 1) * LANES]

    def make_group(kind, i):
        if by_owner and (kind, i) in group_of:
            for at in group_of.pop((kind, i)):
                make(at)
                made.append(places[at])

    made = []
    if not by_owner:
        for at in range(pieces):
            make(at)
        made += places

    def block(o, step1, step2, step3):
        first, second, third = orders[o]
        owner = dp + moved(step1, first) + moved(step2, second) + moved(step3, third)
        return grad.at[pl.ds(pl.multiple_of(owner * shard_rows + spans[o][0], 8), spans[o][1]), :]

    def base1(o, step1, step2, step3):
        first, second, third = orders[o]
        return ((step1 - 1) * second[0] + step2) * third[0] + step3

    def stage1(o, step1, step2, step3):
        at = base1(o, step1, step2, step3)
        return pltpu.make_async_remote_copy(
            src_ref=block(o, step1, step2, step3), dst_ref=got1[o].at[at], send_sem=send1[o].at[at], recv_sem=recv1[o].at[at],
            device_id=(dp + moved(step1, orders[o][0]), section), device_id_type=MESH)

    def stage2(o, step2, step3):
        at = (step2 - 1) * orders[o][2][0] + step3
        return pltpu.make_async_remote_copy(
            src_ref=block(o, 0, step2, step3), dst_ref=got2[o].at[at], send_sem=send2[o].at[at], recv_sem=recv2[o].at[at],
            device_id=(dp + moved(step2, orders[o][1]), section), device_id_type=MESH)

    def stage3(o, step3):
        at = step3 - 1
        return pltpu.make_async_remote_copy(
            src_ref=block(o, 0, 0, step3), dst_ref=got3[o].at[at], send_sem=send3[o].at[at], recv_sem=recv3[o].at[at],
            device_id=(dp + moved(step3, orders[o][2]), section), device_id_type=MESH)

    started = []

    def start(copy):
        copy.start()
        started.append(copy)

    def arrived1(o, step2, step3):
        total = block(o, 0, step2, step3)[...]
        for step1 in range(1, orders[o][0][0]):
            stage1(o, step1, step2, step3).wait_recv()
            total += got1[o][base1(o, step1, step2, step3)]
        return total

    def arrived2(o, step3):
        total = arrived1(o, 0, step3)
        for step2 in range(1, orders[o][1][0]):
            stage2(o, step2, step3).wait_recv()
            total += got2[o][(step2 - 1) * orders[o][2][0] + step3]
        return total

    def send_forward(i):
        if i < len(steps3):
            for o in range(2):
                for step1 in range(1, orders[o][0][0]):
                    for step2 in range(1, orders[o][1][0]):
                        start(stage1(o, step1, step2, steps3[i]))

    def send_own(i):
        if i < len(steps3):
            for o in range(2):
                for step1 in range(1, orders[o][0][0]):
                    start(stage1(o, step1, 0, steps3[i]))

    def send_second(i):
        for o in range(2):
            for step2 in range(1, orders[o][1][0]):
                block(o, 0, step2, steps3[i])[...] = arrived1(o, step2, steps3[i])
                start(stage2(o, step2, steps3[i]))

    def send_third(i):
        for o in range(2):
            block(o, 0, 0, steps3[i])[...] = arrived2(o, steps3[i])
            start(stage3(o, steps3[i]))

    late = range(2, len(spans))

    def late_first(step2, step3, step1):
        for o in late:
            if step1:
                start(stage1(o, step1, *((step2, step3) if orders[o][1] is digits[0] else (step3, step2))))

    def late_second():
        for o in late:
            for step2 in range(1, orders[o][1][0]):
                for step3 in reversed(range(orders[o][2][0])):
                    block(o, 0, step2, step3)[...] = arrived1(o, step2, step3)
                    start(stage2(o, step2, step3))

    def late_third():
        for o in late:
            for step3 in range(1, orders[o][2][0]):
                block(o, 0, 0, step3)[...] = arrived2(o, step3)
                start(stage3(o, step3))

    def send_late():
        while made:
            late_first(*made.pop(0))

    end = len(steps3) - 1
    make_group("forward", 0)
    send_forward(0)
    make_group("own", 0)
    send_own(0)
    send_late()
    make_group("forward", 1)
    if end > 1:
        send_forward(1)
    send_late()
    for kind, i in list(group_of):
        make_group(kind, i)
        send_late()
    for i in range(end + 1):
        if i == end and i:
            send_third(i - 1)
        send_second(i)
        if i == end - 1:
            send_forward(end)
        send_own(i + 1)
        if i + 2 < end:
            send_forward(i + 2)
        if 1 <= i < end:
            send_third(i - 1)
        if i == end - 2:
            late_second()
        if i == end - 1:
            late_third()
    if len(steps3) < 3:
        late_second()
    if len(steps3) < 2:
        late_third()
    for o in reversed(range(len(spans))):
        total = arrived2(o, 0)
        for step3 in range(1, orders[o][2][0]):
            stage3(o, step3).wait_recv()
            total += got3[o][step3 - 1]
        out[spans[o][0]:spans[o][0] + spans[o][1], :] = total
    for copy in exchange + started:
        copy.wait_send()


def shards(digits, acts, cotan, counts, weight, moment, second):
    micro = counts.shape[3]
    rows, depth = acts.shape[2], acts.shape[3]
    width = cotan.shape[3]
    shard_rows = weight.shape[1] // LANES
    piece = weight.shape[1] // width
    pieces = depth // piece if piece % LANES == 0 and weight.shape[1] % width == 0 else depth // (2 * LANES)
    orders = axis_orders(digits)
    spans = row_spans(shard_rows)
    orders = orders[:len(spans)]
    counts1 = [(first[0] - 1) * second[0] * third[0] for first, second, third in orders]
    counts2 = [(second[0] - 1) * third[0] for first, second, third in orders]
    counts3 = [third[0] - 1 for first, second, third in orders]

    def buffers(sizes):
        return [pltpu.VMEM((max(size, 1), span[1], LANES), jnp.float32) for size, span in zip(sizes, spans)]

    def semaphores(sizes):
        return [pltpu.SemaphoreType.DMA((max(size, 1),)) for size in sizes]

    hbm = pl.BlockSpec(memory_space=pl.ANY)
    vmem = pl.BlockSpec(memory_space=pltpu.VMEM)
    shard = pl.pallas_call(
        functools.partial(reduce_kernel, digits, micro, pieces),
        out_shape=jax.ShapeDtypeStruct((shard_rows, LANES), jnp.float32),
        in_specs=[hbm, hbm, pl.BlockSpec(memory_space=pltpu.SMEM)],
        out_specs=vmem,
        scratch_shapes=[
            pltpu.VMEM((2, rows, depth), jnp.bfloat16),
            pltpu.VMEM((2, rows, width), jnp.bfloat16),
            pltpu.VMEM((pieces, rows, depth // pieces), jnp.float32),
            pltpu.VMEM((rows, width), jnp.float32),
            pltpu.VMEM((pieces, rows, depth // pieces), jnp.float32),
            pltpu.VMEM((rows, width), jnp.float32),
            pltpu.VMEM((2 * rows, width), jnp.bfloat16),
            pltpu.VMEM((depth * width // LANES, LANES), jnp.float32),
            buffers(counts1), buffers(counts2), buffers(counts3),
            pltpu.SemaphoreType.DMA((3,)), pltpu.SemaphoreType.DMA((pieces + 1,)), pltpu.SemaphoreType.DMA((pieces + 1,)),
            semaphores(counts1), semaphores(counts1), semaphores(counts2), semaphores(counts2),
            semaphores(counts3), semaphores(counts3),
        ],
        compiler_params=pltpu.CompilerParams(collective_id=0, has_side_effects=True),
        name="reduce_grad",
    )(acts[0], cotan[0], counts[0, :, 0, :].T)
    flat = jax.ShapeDtypeStruct((shard_rows, LANES), jnp.float32)
    outs = pl.pallas_call(
        adamw_kernel,
        out_shape=(flat, flat, flat),
        in_specs=[vmem] * 4,
        out_specs=(vmem, vmem, vmem),
        name="adamw",
    )(shard, *(array.reshape(shard_rows, LANES) for array in (weight, moment, second)))
    return tuple(array.reshape(weight.shape) for array in outs)


AXES = {"A": (0, 1), "B": (1, 0), "C": (0, 1), "D": (1, 0)}


def flipped(family, first, second):
    return (first, second) if AXES[family][0] == 0 else (second, first)


def planes_beside(z, planes):
    return [p for p in (z - 1, z + 1) if 0 <= p < planes]


def crossed(c, place, z, planes):
    return tuple(("z", c, *place, z, p) for p in planes_beside(z, planes))


def send_table(z, planes, spans):
    table = {}
    for f, c in spans:
        if f in AXES:
            first, second = AXES[f]
        if f in "AB":
            for k in range(planes):
                for b in range(2):
                    table["1", f, c, b, k] = (first, z, (), flipped(f, 1, b) + (k,))
                table["2", f, c, k] = (second, z, (("1", f, c, 1, k),), flipped(f, 0, 1) + (k,))
                if k != z:
                    table["3", f, c, k] = (2, k, (("1", f, c, 0, k), ("2", f, c, k)), (0, 0, k))
        elif f in "CD":
            for b in range(2):
                place = flipped(f, 1, b)
                table["x", f, c, b] = (first, z, crossed(c, place, z, planes), place + (z,))
            place = flipped(f, 0, 1)
            table["y", f, c] = (second, z, crossed(c, place, z, planes) + (("x", f, c, 1),), place + (z,))
        else:
            for k in range(planes):
                toward = 1 if k > z else -1
                for a in range(2 if k != z else 0):
                    for b in range(2):
                        needs = (("z", c, a, b, k, z - toward),) if 0 <= z - toward < planes else ()
                        table["z", c, a, b, k] = (2, z + toward, needs, (a, b, k))
    return table


def last_needs(f, c, z, planes):
    if f in "AB":
        return (("1", f, c, 0, z), ("2", f, c, z)) + tuple(("3", f, c, p) for p in range(planes) if p != z)
    return crossed(c, (0, 0), z, planes) + (("x", f, c, 0), ("y", f, c))


def wait_groups(z, planes, spans):
    groups = []
    for f, c in spans:
        if f in "AB":
            for k in range(planes):
                groups.append((("1", f, c, 1, k),))
                groups.append((("1", f, c, 0, k), ("2", f, c, k)) if k != z else last_needs(f, c, z, planes))
        elif f in "CD":
            groups += [(("x", f, c, 1),), (("x", f, c, 0), ("y", f, c))]
        else:
            for place in ((0, 0), (0, 1), (1, 0), (1, 1)):
                groups.append(crossed(c, place, z, planes))
                for k in range(planes):
                    before = z - 1 if k > z else z + 1
                    if k != z and 0 <= before < planes:
                        groups.append((("z", c, *place, k, before),))
    return groups


def key_there(key, z):
    return key[:-1] + (z,) if key[0] == "3" else key + (z,) if key[0] == "z" else key


def span_of(key, spans):
    return spans[("Z",) + key[1:2]] if key[0] == "z" else spans[key[1], key[2]]


def spans_of(piece):
    total = sum(CHUNKS["A"]) + sum(CHUNKS["B"]) + sum(sum(pair) for pair in CHUNKS["Z"])
    unit = piece // 8 // total * 8
    spans, at = {}, 0
    for f in "AB":
        for c, size in enumerate(CHUNKS[f]):
            spans[f, c] = (at, size * unit)
            at += size * unit
    for c, (first, second) in enumerate(CHUNKS["Z"]):
        spans["Z", c] = (at, (first + second) * unit)
        if first:
            spans["C", c] = (at, first * unit)
        if second:
            spans["D", c] = (at + first * unit, second * unit)
        at += (first + second) * unit
    return spans


def landing_of(z, planes, spans):
    places, at, groups = {}, 0, wait_groups(z, planes, spans)
    for i, group in enumerate(groups):
        for key in group:
            rows = span_of(key, spans)[1]
            places[key] = (at, rows, i)
            at += rows
    return places, groups, at


def part_groups(pieces):
    groups, at = [], 0
    for size in (1, 1, 1, 1, 2, 2):
        if at + size <= pieces:
            groups.append((at, size))
            at += size
    while at < pieces:
        groups.append((at, min(4, pieces - at)))
        at += groups[-1][1]
    return groups


def fast_kernel(digits, micro, acts, cotan, counts, weight, moment, second, packed, counts_held, acts_held, cotan_held,
                acts_out, cotan_out, acts_in, cotan_in, rhs, grad, got, state, shard, load_sem, part_send, part_recv,
                send_sem, recv_sem, up_sem):
    section = lax.axis_index("section")
    dp = lax.axis_index("dp")
    mirror = (dp, lax.axis_size("section") - 1 - section)
    planes = digits[2][0]
    strides = [stride for count, stride in digits]
    here = [lax.rem(lax.div(dp, stride), count) for count, stride in digits]
    across = [(1 - 2 * here[axis]) * strides[axis] for axis in range(2)]
    rows, depth = acts.shape[1], acts.shape[2]
    width = cotan.shape[2]
    slots = rows // micro
    pieces = lax.axis_size("dp")
    piece = depth // pieces
    per_row = width // LANES
    spans = spans_of(piece)
    tables = [send_table(z, planes, spans) for z in range(planes)]
    landings = [landing_of(z, planes, spans) for z in range(planes)]
    parts_in = part_groups(pieces)

    loads = [
        pltpu.make_async_copy(cotan, cotan_held, load_sem.at[0]),
        pltpu.make_async_copy(counts, counts_held, load_sem.at[1]),
        pltpu.make_async_copy(acts.at[1], acts_held.at[1], load_sem.at[2]),
        pltpu.make_async_copy(acts.at[0], acts_held.at[0], load_sem.at[3]),
    ]
    state_loads = [pltpu.make_async_copy(array, state.at[i], load_sem.at[4]) for i, array in enumerate((weight, moment, second))]
    for load in loads:
        load.start()

    barrier = pltpu.get_barrier_semaphore()
    pl.semaphore_signal(barrier, inc=1, device_id=mirror, device_id_type=MESH)
    for axis in range(2):
        @pl.when(here[axis] == 0)
        def greet():
            pl.semaphore_signal(barrier, inc=1, device_id=(dp + across[axis], section), device_id_type=MESH)
    for step in range(1, planes):
        @pl.when(here[2] + step < planes)
        def greet_plane():
            pl.semaphore_signal(barrier, inc=1, device_id=(dp + step * strides[2], section), device_id_type=MESH)

    def masked(k):
        parts = []
        for b in range(micro):
            block = cotan_held[k, b * slots:(b + 1) * slots, :].astype(jnp.float32)
            place = lax.broadcasted_iota(jnp.int32, (slots, width), 0)
            parts.append(jnp.where(place < counts_held[b, k], block, 0.0))
        return parts[0] if micro == 1 else jnp.concatenate(parts, axis=0)

    def to_mirror(src, dst, sent, received):
        return pltpu.make_async_remote_copy(
            src_ref=src, dst_ref=dst, send_sem=part_send.at[sent], recv_sem=part_recv.at[received],
            device_id=mirror, device_id_type=MESH)

    cotan_swap = to_mirror(cotan_out, cotan_in, 0, 0)
    group_at = {at + i: g for g, (at, size) in enumerate(parts_in) for i in range(size)}
    acts_swap = [to_mirror(acts_out.at[at], acts_in.at[at], 1, 1 + group_at[at]) for at in range(pieces)]
    loads[0].wait()
    loads[1].wait()
    cotan_out[...] = masked(1)
    pl.semaphore_wait(barrier, 1 + here[0] + here[1] + here[2])
    cotan_swap.start()
    rhs[0:rows, :] = masked(0).astype(jnp.bfloat16)
    for axis in range(2):
        @pl.when(here[axis] == 1)
        def answer():
            pl.semaphore_signal(up_sem.at[axis], inc=1, device_id=(dp + across[axis], section), device_id_type=MESH)
    for step in range(1, planes):
        @pl.when(here[2] >= step)
        def answer_plane():
            pl.semaphore_signal(up_sem.at[1 + step], inc=1, device_id=(dp - step * strides[2], section), device_id_type=MESH)
    loads[2].wait()

    def run(z):
        table = tables[z]
        places, groups, unused = landings[z]
        order = ORDERS[z]
        owners = []
        for key in order:
            if table[key][3] not in owners:
                owners.append(table[key][3])
        owners.append((0, 0, z))

        def owner_index(owner):
            return dp + owner[0] * across[0] + owner[1] * across[1] + (owner[2] - z) * strides[2]

        def columns(owner):
            return pl.ds(pl.multiple_of(owner_index(owner) * piece, LANES), piece)

        for at, owner in enumerate(owners):
            acts_out[at] = acts_held[1, :, columns(owner)].astype(jnp.float32)
            acts_swap[at].start()
        for load in state_loads:
            load.start()
        loads[3].wait()
        cotan_swap.wait_recv()
        rhs[rows:2 * rows, :] = cotan_in[...].astype(jnp.bfloat16)
        swapped = set()

        def make(at):
            g = group_at[at]
            if g not in swapped:
                swapped.add(g)
                part = acts_in.at[pl.ds(*parts_in[g])]
                to_mirror(part, part, 1, 1 + g).wait_recv()
            lhs = jnp.concatenate([acts_held[0, :, columns(owners[at])], acts_in[at].astype(jnp.bfloat16)], axis=0)
            first = pl.multiple_of(owner_index(owners[at]) * piece, piece)
            grad[pl.ds(first, piece), :] = lax.dot_general(
                lhs, rhs[...], (((0,), (0,)), ((), ())), preferred_element_type=jnp.float32)

        def block(owner, span):
            return pl.ds(pl.multiple_of(owner_index(owner) * piece + span[0], 8), span[1])

        def copy_of(key):
            axis, target, needs, owner = table[key]
            place, size, at = landings[target][0][key_there(key, z)]
            device = dp + across[axis] if axis < 2 else dp + (target - z) * strides[2]
            return pltpu.make_async_remote_copy(
                src_ref=grad.at[block(owner, span_of(key, spans)), :], dst_ref=got.at[pl.ds(place, size), :],
                send_sem=send_sem.at[0], recv_sem=recv_sem.at[at], device_id=(device, section), device_id_type=MESH)

        landed = set()

        def arrived(key, span):
            place, size, at = places[key]
            if at not in landed:
                landed.add(at)
                start = places[groups[at][0]][0]
                whole = got.at[pl.ds(start, sum(places[k][1] for k in groups[at])), :]
                pltpu.make_async_remote_copy(
                    src_ref=whole, dst_ref=whole, send_sem=send_sem.at[0], recv_sem=recv_sem.at[at],
                    device_id=mirror, device_id_type=MESH).wait_recv()
            place += span[0] - span_of(key, spans)[0]
            return got[place:place + span[1], :]

        met, done = set(), 0
        for key in order:
            axis, target, needs, owner = table[key]
            while done <= owners.index(owner):
                make(done)
                done += 1
            if needs:
                span = span_of(key, spans)
                at = block(owner, span)
                total = grad[at, :]
                for need in needs:
                    total += arrived(need, span)
                grad[at, :] = total
            if axis < 2 and axis not in met:
                met.add(axis)

                @pl.when(here[axis] == 0)
                def wait_up():
                    pl.semaphore_wait(up_sem.at[axis], 1)
            if axis == 2 and target > z and 1 + target - z not in met:
                met.add(1 + target - z)
                pl.semaphore_wait(up_sem.at[1 + target - z], 1)
            copy_of(key).start()
        while done < pieces:
            make(done)
            done += 1
        pltpu.make_async_copy(state, state, load_sem.at[4]).wait()
        for f, c in LASTS[z]:
            span = spans[f, c]
            total = grad[block((0, 0, z), span), :]
            for need in last_needs(f, c, z, planes):
                total += arrived(need, span)
            for part in range(per_row):
                shard[pl.ds(span[0] * per_row + part, span[1], stride=per_row), :] = total[:, part * LANES:(part + 1) * LANES]
            flat = slice(span[0] * per_row, (span[0] + span[1]) * per_row)
            updated = adamw_shard(shard[flat, :], state[0, flat, :], state[1, flat, :], state[2, flat, :])
            for i in range(3):
                packed[i, flat, :] = updated[i]
        cotan_swap.wait_send()
        to_mirror(acts_out, acts_in, 1, 1).wait_send()
        sent = grad.at[pl.ds(0, sum(span_of(key, spans)[1] for key in order)), :]
        pltpu.make_async_remote_copy(
            src_ref=sent, dst_ref=sent, send_sem=send_sem.at[0], recv_sem=recv_sem.at[0],
            device_id=mirror, device_id_type=MESH).wait_send()

    for z in range(planes):
        pl.when(here[2] == z)(functools.partial(run, z))


def put_kernel(packed, new_weight, new_moment, new_second, sem):
    copies = [pltpu.make_async_copy(packed.at[i], out, sem.at[i]) for i, out in enumerate((new_weight, new_moment, new_second))]
    for copy in copies:
        copy.start()
    for copy in copies:
        copy.wait()


def fast_fits(digits, acts, cotan, weight):
    planes, depth, width = digits[2][0], acts.shape[3], cotan.shape[3]
    piece = depth // (4 * planes)
    unit = spans_of(piece)
    whole = sum(rows for (f, c), (at, rows) in unit.items() if f in "ABZ")
    return (digits[0][0] == 2 and digits[1][0] == 2 and planes == len(ORDERS) and piece % LANES == 0 and whole == piece
            and width % LANES == 0 and piece * width == weight.shape[1])


def fast_shards(digits, acts, cotan, counts, weight, moment, second):
    micro = counts.shape[3]
    rows, depth = acts.shape[2], acts.shape[3]
    width = cotan.shape[3]
    shard_rows = weight.shape[1] // LANES
    planes = digits[2][0]
    pieces = 4 * planes
    spans = spans_of(depth // pieces)
    landings = [landing_of(z, planes, spans) for z in range(planes)]
    received = max(len(groups) for places, groups, total in landings)
    space = max(total for places, groups, total in landings)
    hbm = pl.BlockSpec(memory_space=pl.ANY)
    vmem = pl.BlockSpec(memory_space=pltpu.VMEM)
    flat = (shard_rows, LANES)
    packed = pl.pallas_call(
        functools.partial(fast_kernel, digits, micro),
        out_shape=pltpu.VMEM((3, *flat), jnp.float32),
        in_specs=[hbm] * 6,
        out_specs=vmem,
        scratch_shapes=[
            pltpu.SMEM((micro, 2), jnp.int32),
            pltpu.VMEM((2, rows, depth), jnp.bfloat16),
            pltpu.VMEM((2, rows, width), jnp.bfloat16),
            pltpu.VMEM((pieces, rows, depth // pieces), jnp.float32),
            pltpu.VMEM((rows, width), jnp.float32),
            pltpu.VMEM((pieces, rows, depth // pieces), jnp.float32),
            pltpu.VMEM((rows, width), jnp.float32),
            pltpu.VMEM((2 * rows, width), jnp.bfloat16),
            pltpu.VMEM((depth, width), jnp.float32),
            pltpu.VMEM((space, width), jnp.float32),
            pltpu.VMEM((3, *flat), jnp.float32),
            pltpu.VMEM(flat, jnp.float32),
            pltpu.SemaphoreType.DMA((5,)), pltpu.SemaphoreType.DMA((2,)), pltpu.SemaphoreType.DMA((1 + len(part_groups(pieces)),)),
            pltpu.SemaphoreType.DMA((1,)), pltpu.SemaphoreType.DMA((received,)), pltpu.SemaphoreType.REGULAR((1 + planes,)),
        ],
        compiler_params=pltpu.CompilerParams(collective_id=0, has_side_effects=True, vmem_limit_bytes=66 * 10**6),
        name="reduce_adamw",
    )(acts[0], cotan[0], counts[0, :, 0, :].T, *(array.reshape(flat) for array in (weight, moment, second)))
    outs = pl.pallas_call(
        put_kernel,
        out_shape=(jax.ShapeDtypeStruct(flat, jnp.float32),) * 3,
        in_specs=[vmem],
        out_specs=(hbm, hbm, hbm),
        scratch_shapes=[pltpu.SemaphoreType.DMA((3,))],
        name="put",
    )(pltpu.with_memory_space_constraint(packed, pltpu.VMEM))
    return tuple(array.reshape(weight.shape) for array in outs)


def solution(mesh):
    in_specs = (
        P("section", None, "dp", None),
        P("section", None, "dp", None),
        P("section", None, "dp", None),
        P("section", "dp"),
        P("section", "dp"),
        P("section", "dp"),
    )
    out_specs = (P("section", "dp"), P("section", "dp"), P("section", "dp"))
    digits = dp_digits(mesh)

    def body(acts, cotan, counts, weight, moment, second):
        form = fast_shards if fast_fits(digits, acts, cotan, weight) else shards
        return form(digits, acts, cotan, counts, weight, moment, second)

    return jax.shard_map(body, mesh=mesh, in_specs=in_specs, out_specs=out_specs, check_vma=False)
```

```python
import functools
import jax
import jax.numpy as jnp
from jax import lax
from jax.experimental import pallas as pl
from jax.experimental.pallas import tpu as pltpu
from jax.sharding import PartitionSpec as P

LANES = 128
MESH = pl.DeviceIdType.MESH


CHUNKS = {"A": (6,), "B": (6,), "Z": ((2, 2),)}
RELAYS = ((3, 0), (0, 3))
LASTS = (
    (("C", 0), ("D", 0), ("A", 0), ("B", 0)),
    (("C", 0), ("D", 0), ("A", 0), ("B", 0)),
    (("C", 0), ("D", 0), ("A", 0), ("B", 0)),
    (("C", 0), ("D", 0), ("A", 0), ("B", 0)),
)
ORDERS = (
    (
        ("z", 0, 1, 1, 3), ("1", "B", 0, 1, 3), ("1", "A", 0, 1, 3), ("1", "A", 0, 1, 0), ("1", "A", 0, 1, 2),
        ("1", "B", 0, 0, 3), ("z", 0, 0, 1, 3), ("1", "A", 0, 0, 3), ("1", "B", 0, 1, 2), ("z", 0, 1, 0, 3),
        ("1", "A", 0, 0, 2), ("z", 0, 0, 0, 3), ("z", 0, 0, 1, 2), ("z", 0, 0, 0, 2), ("1", "B", 0, 0, 1), ("z", 0, 1, 1, 2),
        ("z", 0, 1, 0, 2), ("z", 0, 1, 0, 1), ("2", "B", 0, 3), ("z", 0, 1, 1, 1), ("1", "A", 0, 0, 1), ("1", "B", 0, 1, 0),
        ("z", 0, 0, 1, 1), ("1", "B", 0, 1, 1), ("2", "A", 0, 2), ("1", "A", 0, 1, 1), ("2", "A", 0, 3), ("1", "B", 0, 0, 2),
        ("z", 0, 0, 0, 1), ("2", "B", 0, 2), ("x", "C", 0, 1), ("2", "B", 0, 1), ("3", "B", 0, 3), ("1", "A", 0, 0, 0),
        ("x", "D", 0, 1), ("1", "B", 0, 0, 0), ("3", "A", 0, 2), ("2", "A", 0, 1), ("3", "A", 0, 3), ("2", "B", 0, 0),
        ("y", "D", 0), ("2", "A", 0, 0), ("x", "D", 0, 0), ("3", "B", 0, 2), ("y", "C", 0), ("x", "C", 0, 0), ("3", "B", 0, 1),
        ("3", "A", 0, 1),
    ),
    (
        ("1", "B", 0, 1, 3), ("1", "A", 0, 1, 0), ("1", "B", 0, 1, 2), ("1", "B", 0, 1, 0), ("1", "A", 0, 1, 1),
        ("1", "B", 0, 1, 1), ("z", 0, 1, 1, 3), ("1", "A", 0, 1, 2), ("2", "A", 0, 0), ("1", "A", 0, 0, 0),
        ("1", "B", 0, 0, 2), ("z", 0, 0, 1, 3), ("2", "B", 0, 3), ("z", 0, 0, 0, 3), ("z", 0, 1, 0, 3), ("z", 0, 0, 1, 2),
        ("2", "A", 0, 2), ("2", "B", 0, 2), ("1", "A", 0, 1, 3), ("z", 0, 0, 0, 2), ("1", "B", 0, 0, 0), ("z", 0, 1, 1, 0),
        ("1", "A", 0, 0, 2), ("2", "B", 0, 0), ("z", 0, 1, 1, 2), ("z", 0, 1, 0, 0), ("z", 0, 0, 1, 0), ("1", "B", 0, 0, 3),
        ("1", "A", 0, 0, 3), ("3", "A", 0, 0), ("z", 0, 1, 0, 2), ("x", "D", 0, 1), ("3", "B", 0, 2), ("x", "C", 0, 1),
        ("2", "A", 0, 3), ("1", "B", 0, 0, 1), ("3", "A", 0, 2), ("x", "C", 0, 0), ("3", "B", 0, 0), ("3", "B", 0, 3),
        ("y", "D", 0), ("1", "A", 0, 0, 1), ("x", "D", 0, 0), ("y", "C", 0), ("3", "A", 0, 3), ("2", "A", 0, 1),
        ("z", 0, 0, 0, 0), ("2", "B", 0, 1),
    ),
    (
        ("1", "B", 0, 1, 1), ("1", "A", 0, 1, 1), ("1", "B", 0, 1, 3), ("1", "B", 0, 1, 0), ("1", "A", 0, 0, 0),
        ("1", "A", 0, 1, 0), ("1", "B", 0, 0, 0), ("1", "A", 0, 0, 1), ("z", 0, 1, 1, 0), ("2", "A", 0, 1),
        ("1", "B", 0, 0, 3), ("z", 0, 0, 1, 0), ("1", "A", 0, 1, 3), ("1", "A", 0, 1, 2), ("z", 0, 1, 0, 0), ("z", 0, 1, 1, 1),
        ("z", 0, 0, 1, 1), ("2", "B", 0, 0), ("2", "B", 0, 3), ("z", 0, 1, 1, 3), ("2", "A", 0, 0), ("z", 0, 0, 0, 1),
        ("2", "B", 0, 1), ("z", 0, 1, 0, 1), ("1", "B", 0, 1, 2), ("1", "B", 0, 0, 1), ("1", "A", 0, 0, 3), ("z", 0, 0, 0, 3),
        ("2", "A", 0, 3), ("z", 0, 0, 1, 3), ("3", "A", 0, 1), ("1", "A", 0, 0, 2), ("z", 0, 0, 0, 0), ("z", 0, 1, 0, 3),
        ("3", "B", 0, 0), ("3", "A", 0, 0), ("3", "B", 0, 3), ("x", "C", 0, 1), ("x", "D", 0, 1), ("3", "B", 0, 1),
        ("2", "A", 0, 2), ("3", "A", 0, 3), ("2", "B", 0, 2), ("1", "B", 0, 0, 2), ("x", "C", 0, 0), ("y", "D", 0),
        ("x", "D", 0, 0), ("y", "C", 0),
    ),
    (
        ("z", 0, 1, 1, 0), ("1", "B", 0, 1, 0), ("1", "A", 0, 1, 0), ("1", "B", 0, 0, 1), ("z", 0, 0, 1, 0),
        ("1", "B", 0, 1, 1), ("z", 0, 1, 0, 0), ("1", "B", 0, 0, 0), ("1", "A", 0, 1, 2), ("z", 0, 1, 1, 1),
        ("1", "A", 0, 1, 1), ("z", 0, 0, 1, 1), ("2", "B", 0, 0), ("2", "A", 0, 0), ("1", "B", 0, 1, 3), ("1", "B", 0, 1, 2),
        ("z", 0, 0, 0, 1), ("1", "A", 0, 0, 0), ("2", "A", 0, 2), ("z", 0, 1, 0, 1), ("z", 0, 0, 0, 0), ("z", 0, 1, 0, 2),
        ("1", "A", 0, 1, 3), ("1", "A", 0, 0, 1), ("1", "A", 0, 0, 2), ("2", "A", 0, 1), ("3", "B", 0, 0), ("3", "A", 0, 0),
        ("z", 0, 1, 1, 2), ("2", "B", 0, 1), ("z", 0, 0, 0, 2), ("x", "C", 0, 1), ("x", "D", 0, 1), ("1", "B", 0, 0, 2),
        ("z", 0, 0, 1, 2), ("1", "B", 0, 0, 3), ("2", "B", 0, 2), ("2", "B", 0, 3), ("2", "A", 0, 3), ("3", "A", 0, 2),
        ("3", "A", 0, 1), ("y", "C", 0), ("3", "B", 0, 1), ("1", "A", 0, 0, 3), ("y", "D", 0), ("x", "C", 0, 0),
        ("x", "D", 0, 0), ("3", "B", 0, 2),
    ),
)


def adamw_shard(grad, weight_now, moment_now, second_now):
    new_m = 0.9 * moment_now + 0.1 * grad
    new_v = 0.95 * second_now + 0.05 * grad * grad
    corr_m = new_m / (1.0 - 0.9**10)
    corr_v = new_v / (1.0 - 0.95**10)
    new_w = weight_now - 0.01 * (corr_m / (jnp.sqrt(corr_v) + 1e-08) + 0.1 * weight_now)
    return (new_w, new_m, new_v)


def adamw_kernel(grad, weight, moment, second, new_weight, new_moment, new_second):
    new_w, new_m, new_v = adamw_shard(grad[...], weight[...], moment[...], second[...])
    new_weight[...] = new_w
    new_moment[...] = new_m
    new_second[...] = new_v


def dp_digits(mesh):
    size = mesh.shape["dp"]
    line = mesh.devices.reshape(size, -1)[:, 0]
    digits = []
    if hasattr(line[0], "coords"):
        for axis in range(3):
            at = [device.coords[axis] for device in line]
            if len(set(at)) > 1:
                digits.append((len(set(at)), next(j for j in range(size) if at[j] != at[0])))
    total = 1
    for count, stride in digits:
        total *= count
    if total != size:
        digits = [(size, 1)] if size > 1 else []
    digits.sort()
    return [(1, 1)] * (3 - len(digits)) + digits


def axis_orders(digits):
    a, b, c = digits
    return [(a, b, c), (b, a, c), (c, a, b), (c, b, a)]


def row_spans(shard_rows):
    late = shard_rows // 128 * 8
    early = (shard_rows - 2 * late) // 2
    spans = [(0, early), (early, early), (2 * early, late), (2 * early + late, late)]
    return spans[:4 if late else 2]


def reduce_kernel(digits, micro, pieces, acts, cotan, counts, out, acts_held, cotan_held, acts_out, cotan_out, acts_in, cotan_in, rhs,
                  grad, got1, got2, got3, load_sem, part_send, part_recv, send1, recv1, send2, recv2, send3, recv3):
    sections = lax.axis_size("section")
    section = lax.axis_index("section")
    dp = lax.axis_index("dp")
    mirror = sections - 1 - section

    def moved(step, digit):
        count, stride = digit
        mine = lax.rem(lax.div(dp, stride), count)
        return (lax.rem(mine + step, count) - mine) * stride

    peers = [(dp, mirror)]
    for digit in digits:
        peers += [(dp + moved(step, digit), section) for step in range(1, digit[0])]
    barrier = pltpu.get_barrier_semaphore()
    for peer in peers:
        pl.semaphore_signal(barrier, inc=1, device_id=peer, device_id_type=MESH)
    loads = [
        pltpu.make_async_copy(cotan, cotan_held, load_sem.at[0]),
        pltpu.make_async_copy(acts.at[1], acts_held.at[1], load_sem.at[1]),
        pltpu.make_async_copy(acts.at[0], acts_held.at[0], load_sem.at[2]),
    ]
    for load in loads:
        load.start()

    rows, depth = acts.shape[1], acts.shape[2]
    width = cotan.shape[2]
    slots = rows // micro
    shard_rows = out.shape[0]
    orders = axis_orders(digits)
    spans = row_spans(shard_rows)
    last = digits[2]
    per_row = width // LANES

    def masked(k):
        parts = []
        for b in range(micro):
            block = cotan_held[k, b * slots:(b + 1) * slots, :].astype(jnp.float32)
            place = lax.broadcasted_iota(jnp.int32, (slots, width), 0)
            parts.append(jnp.where(place < counts[b, k], block, 0.0))
        return parts[0] if micro == 1 else jnp.concatenate(parts, axis=0)

    steps3 = sorted(range(1, last[0]), key=lambda step: -min(step, last[0] - step)) + [0]
    piece = depth // pieces
    by_owner = pieces == lax.axis_size("dp")
    kinds = {"forward": [], "own": [], "mine": []}
    for step_a in range(digits[0][0]):
        for step_b in range(digits[1][0]):
            kind = "forward" if step_a and step_b else "own" if step_a or step_b else "mine"
            kinds[kind].append((step_a, step_b))
    groups = [("forward", 0), ("own", 0), ("forward", 1)]
    groups += [(kind, i) for i in range(len(steps3)) for kind in ("own", "forward", "mine") if (kind, i) not in groups]
    owners, places, group_of = [], [], {}
    for kind, i in groups:
        if i < len(steps3):
            group_of[kind, i] = range(len(owners), len(owners) + len(kinds[kind]))
            for step_a, step_b in kinds[kind]:
                places.append((step_a, step_b, steps3[i]))
                owners.append(dp + moved(step_a, digits[0]) + moved(step_b, digits[1]) + moved(steps3[i], last))
    if not by_owner:
        owners = list(range(pieces))

    def columns(at):
        start = owners[at] * piece
        return pl.ds(start if isinstance(start, int) else pl.multiple_of(start, LANES), piece)

    def to_mirror(src, dst, at):
        return pltpu.make_async_remote_copy(
            src_ref=src, dst_ref=dst, send_sem=part_send.at[at], recv_sem=part_recv.at[at],
            device_id=(dp, mirror), device_id_type=MESH)

    exchange = [to_mirror(acts_out.at[at], acts_in.at[at], at) for at in range(pieces)]
    exchange.append(to_mirror(cotan_out, cotan_in, pieces))
    loads[0].wait()
    cotan_out[...] = masked(1)
    rhs[0:rows, :] = masked(0).astype(jnp.bfloat16)
    loads[1].wait()
    for at in range(pieces):
        acts_out[at] = acts_held[1, :, columns(at)].astype(jnp.float32)
    pl.semaphore_wait(barrier, len(peers))
    exchange[pieces].start()
    for copy in exchange[:pieces]:
        copy.start()
    loads[2].wait()
    exchange[pieces].wait_recv()
    rhs[rows:2 * rows, :] = cotan_in[...].astype(jnp.bfloat16)

    def make(at):
        exchange[at].wait_recv()
        lhs = jnp.concatenate([acts_held[0, :, columns(at)], acts_in[at].astype(jnp.bfloat16)], axis=0)
        product = lax.dot_general(lhs, rhs[...], (((0,), (0,)), ((), ())), preferred_element_type=jnp.float32)
        first = owners[at] * (piece * per_row)
        if not isinstance(first, int):
            first = pl.multiple_of(first, 8)
        for c in range(per_row):
            grad[pl.ds(first + c, piece, stride=per_row), :] = product[:, c * LANES:(c + 1) * LANES]

    def make_group(kind, i):
        if by_owner and (kind, i) in group_of:
            for at in group_of.pop((kind, i)):
                make(at)
                made.append(places[at])

    made = []
    if not by_owner:
        for at in range(pieces):
            make(at)
        made += places

    def block(o, step1, step2, step3):
        first, second, third = orders[o]
        owner = dp + moved(step1, first) + moved(step2, second) + moved(step3, third)
        return grad.at[pl.ds(pl.multiple_of(owner * shard_rows + spans[o][0], 8), spans[o][1]), :]

    def base1(o, step1, step2, step3):
        first, second, third = orders[o]
        return ((step1 - 1) * second[0] + step2) * third[0] + step3

    def stage1(o, step1, step2, step3):
        at = base1(o, step1, step2, step3)
        return pltpu.make_async_remote_copy(
            src_ref=block(o, step1, step2, step3), dst_ref=got1[o].at[at], send_sem=send1[o].at[at], recv_sem=recv1[o].at[at],
            device_id=(dp + moved(step1, orders[o][0]), section), device_id_type=MESH)

    def stage2(o, step2, step3):
        at = (step2 - 1) * orders[o][2][0] + step3
        return pltpu.make_async_remote_copy(
            src_ref=block(o, 0, step2, step3), dst_ref=got2[o].at[at], send_sem=send2[o].at[at], recv_sem=recv2[o].at[at],
            device_id=(dp + moved(step2, orders[o][1]), section), device_id_type=MESH)

    def stage3(o, step3):
        at = step3 - 1
        return pltpu.make_async_remote_copy(
            src_ref=block(o, 0, 0, step3), dst_ref=got3[o].at[at], send_sem=send3[o].at[at], recv_sem=recv3[o].at[at],
            device_id=(dp + moved(step3, orders[o][2]), section), device_id_type=MESH)

    started = []

    def start(copy):
        copy.start()
        started.append(copy)

    def arrived1(o, step2, step3):
        total = block(o, 0, step2, step3)[...]
        for step1 in range(1, orders[o][0][0]):
            stage1(o, step1, step2, step3).wait_recv()
            total += got1[o][base1(o, step1, step2, step3)]
        return total

    def arrived2(o, step3):
        total = arrived1(o, 0, step3)
        for step2 in range(1, orders[o][1][0]):
            stage2(o, step2, step3).wait_recv()
            total += got2[o][(step2 - 1) * orders[o][2][0] + step3]
        return total

    def send_forward(i):
        if i < len(steps3):
            for o in range(2):
                for step1 in range(1, orders[o][0][0]):
                    for step2 in range(1, orders[o][1][0]):
                        start(stage1(o, step1, step2, steps3[i]))

    def send_own(i):
        if i < len(steps3):
            for o in range(2):
                for step1 in range(1, orders[o][0][0]):
                    start(stage1(o, step1, 0, steps3[i]))

    def send_second(i):
        for o in range(2):
            for step2 in range(1, orders[o][1][0]):
                block(o, 0, step2, steps3[i])[...] = arrived1(o, step2, steps3[i])
                start(stage2(o, step2, steps3[i]))

    def send_third(i):
        for o in range(2):
            block(o, 0, 0, steps3[i])[...] = arrived2(o, steps3[i])
            start(stage3(o, steps3[i]))

    late = range(2, len(spans))

    def late_first(step2, step3, step1):
        for o in late:
            if step1:
                start(stage1(o, step1, *((step2, step3) if orders[o][1] is digits[0] else (step3, step2))))

    def late_second():
        for o in late:
            for step2 in range(1, orders[o][1][0]):
                for step3 in reversed(range(orders[o][2][0])):
                    block(o, 0, step2, step3)[...] = arrived1(o, step2, step3)
                    start(stage2(o, step2, step3))

    def late_third():
        for o in late:
            for step3 in range(1, orders[o][2][0]):
                block(o, 0, 0, step3)[...] = arrived2(o, step3)
                start(stage3(o, step3))

    def send_late():
        while made:
            late_first(*made.pop(0))

    end = len(steps3) - 1
    make_group("forward", 0)
    send_forward(0)
    make_group("own", 0)
    send_own(0)
    send_late()
    make_group("forward", 1)
    if end > 1:
        send_forward(1)
    send_late()
    for kind, i in list(group_of):
        make_group(kind, i)
        send_late()
    for i in range(end + 1):
        if i == end and i:
            send_third(i - 1)
        send_second(i)
        if i == end - 1:
            send_forward(end)
        send_own(i + 1)
        if i + 2 < end:
            send_forward(i + 2)
        if 1 <= i < end:
            send_third(i - 1)
        if i == end - 2:
            late_second()
        if i == end - 1:
            late_third()
    if len(steps3) < 3:
        late_second()
    if len(steps3) < 2:
        late_third()
    for o in reversed(range(len(spans))):
        total = arrived2(o, 0)
        for step3 in range(1, orders[o][2][0]):
            stage3(o, step3).wait_recv()
            total += got3[o][step3 - 1]
        out[spans[o][0]:spans[o][0] + spans[o][1], :] = total
    for copy in exchange + started:
        copy.wait_send()


def shards(digits, acts, cotan, counts, weight, moment, second):
    micro = counts.shape[3]
    rows, depth = acts.shape[2], acts.shape[3]
    width = cotan.shape[3]
    shard_rows = weight.shape[1] // LANES
    piece = weight.shape[1] // width
    pieces = depth // piece if piece % LANES == 0 and weight.shape[1] % width == 0 else depth // (2 * LANES)
    orders = axis_orders(digits)
    spans = row_spans(shard_rows)
    orders = orders[:len(spans)]
    counts1 = [(first[0] - 1) * second[0] * third[0] for first, second, third in orders]
    counts2 = [(second[0] - 1) * third[0] for first, second, third in orders]
    counts3 = [third[0] - 1 for first, second, third in orders]

    def buffers(sizes):
        return [pltpu.VMEM((max(size, 1), span[1], LANES), jnp.float32) for size, span in zip(sizes, spans)]

    def semaphores(sizes):
        return [pltpu.SemaphoreType.DMA((max(size, 1),)) for size in sizes]

    hbm = pl.BlockSpec(memory_space=pl.ANY)
    vmem = pl.BlockSpec(memory_space=pltpu.VMEM)
    shard = pl.pallas_call(
        functools.partial(reduce_kernel, digits, micro, pieces),
        out_shape=jax.ShapeDtypeStruct((shard_rows, LANES), jnp.float32),
        in_specs=[hbm, hbm, pl.BlockSpec(memory_space=pltpu.SMEM)],
        out_specs=vmem,
        scratch_shapes=[
            pltpu.VMEM((2, rows, depth), jnp.bfloat16),
            pltpu.VMEM((2, rows, width), jnp.bfloat16),
            pltpu.VMEM((pieces, rows, depth // pieces), jnp.float32),
            pltpu.VMEM((rows, width), jnp.float32),
            pltpu.VMEM((pieces, rows, depth // pieces), jnp.float32),
            pltpu.VMEM((rows, width), jnp.float32),
            pltpu.VMEM((2 * rows, width), jnp.bfloat16),
            pltpu.VMEM((depth * width // LANES, LANES), jnp.float32),
            buffers(counts1), buffers(counts2), buffers(counts3),
            pltpu.SemaphoreType.DMA((3,)), pltpu.SemaphoreType.DMA((pieces + 1,)), pltpu.SemaphoreType.DMA((pieces + 1,)),
            semaphores(counts1), semaphores(counts1), semaphores(counts2), semaphores(counts2),
            semaphores(counts3), semaphores(counts3),
        ],
        compiler_params=pltpu.CompilerParams(collective_id=0, has_side_effects=True),
        name="reduce_grad",
    )(acts[0], cotan[0], counts[0, :, 0, :].T)
    flat = jax.ShapeDtypeStruct((shard_rows, LANES), jnp.float32)
    outs = pl.pallas_call(
        adamw_kernel,
        out_shape=(flat, flat, flat),
        in_specs=[vmem] * 4,
        out_specs=(vmem, vmem, vmem),
        name="adamw",
    )(shard, *(array.reshape(shard_rows, LANES) for array in (weight, moment, second)))
    return tuple(array.reshape(weight.shape) for array in outs)


AXES = {"A": (0, 1), "B": (1, 0), "C": (0, 1), "D": (1, 0)}


def flipped(family, first, second):
    return (first, second) if AXES[family][0] == 0 else (second, first)


def planes_beside(z, planes):
    return [p for p in (z - 1, z + 1) if 0 <= p < planes]


def crossed(c, place, z, planes):
    return tuple(("z", c, *place, z, p) for p in planes_beside(z, planes))


def toward(z, k):
    return 1 if k > z else -1


def third_needs(f, c, k, z):
    before = z - toward(z, k)
    return (("1", f, c, 0, k), ("2", f, c, k)) + ((("r", f, c, k, before),) if (before, k) in RELAYS else ())


def send_table(z, planes, spans):
    table = {}
    for f, c in spans:
        if f in AXES:
            first, second = AXES[f]
        if f in "AB":
            for k in range(planes):
                for b in range(2):
                    table["1", f, c, b, k] = (first, z, (), flipped(f, 1, b) + (k,))
                table["2", f, c, k] = (second, z, (("1", f, c, 1, k),), flipped(f, 0, 1) + (k,))
                if k != z:
                    target = z + toward(z, k) if (z, k) in RELAYS else k
                    table["3", f, c, k] = (2, target, third_needs(f, c, k, z), (0, 0, k))
        elif f in "CD":
            for b in range(2):
                place = flipped(f, 1, b)
                table["x", f, c, b] = (first, z, crossed(c, place, z, planes), place + (z,))
            place = flipped(f, 0, 1)
            table["y", f, c] = (second, z, crossed(c, place, z, planes) + (("x", f, c, 1),), place + (z,))
        else:
            for k in range(planes):
                before = z - toward(z, k)
                for a in range(2 if k != z else 0):
                    for b in range(2):
                        needs = (("z", c, a, b, k, before),) if 0 <= before < planes else ()
                        table["z", c, a, b, k] = (2, z + toward(z, k), needs, (a, b, k))
    return table


def last_needs(f, c, z, planes):
    if f in "AB":
        return (("1", f, c, 0, z), ("2", f, c, z)) + tuple(("3", f, c, p) for p in range(planes) if p != z and (p, z) not in RELAYS)
    return crossed(c, (0, 0), z, planes) + (("x", f, c, 0), ("y", f, c))


def wait_groups(z, planes, spans):
    groups = []
    for f, c in spans:
        if f in "AB":
            for k in range(planes):
                groups.append((("1", f, c, 1, k),))
                groups.append(third_needs(f, c, k, z) if k != z else last_needs(f, c, z, planes))
        elif f in "CD":
            groups += [(("x", f, c, 1),), (("x", f, c, 0), ("y", f, c))]
        else:
            for place in ((0, 0), (0, 1), (1, 0), (1, 1)):
                groups.append(crossed(c, place, z, planes))
                for k in range(planes):
                    before = z - toward(z, k)
                    if k != z and 0 <= before < planes:
                        groups.append((("z", c, *place, k, before),))
    return groups


def key_there(key, z):
    if key[0] == "3":
        return ("r",) + key[1:] + (z,) if (z, key[3]) in RELAYS else key[:-1] + (z,)
    return key + (z,) if key[0] == "z" else key


def span_of(key, spans):
    return spans[("Z",) + key[1:2]] if key[0] == "z" else spans[key[1], key[2]]


def spans_of(piece):
    total = sum(CHUNKS["A"]) + sum(CHUNKS["B"]) + sum(sum(pair) for pair in CHUNKS["Z"])
    unit = piece // 8 // total * 8
    spans, at = {}, 0
    for f in "AB":
        for c, size in enumerate(CHUNKS[f]):
            spans[f, c] = (at, size * unit)
            at += size * unit
    for c, (first, second) in enumerate(CHUNKS["Z"]):
        spans["Z", c] = (at, (first + second) * unit)
        if first:
            spans["C", c] = (at, first * unit)
        if second:
            spans["D", c] = (at + first * unit, second * unit)
        at += (first + second) * unit
    return spans


def landing_of(z, planes, spans):
    places, at, groups = {}, 0, wait_groups(z, planes, spans)
    for i, group in enumerate(groups):
        for key in group:
            rows = span_of(key, spans)[1]
            places[key] = (at, rows, i)
            at += rows
    return places, groups, at


def part_groups(pieces):
    groups, at = [], 0
    for size in (1, 1, 1, 1, 2, 2):
        if at + size <= pieces:
            groups.append((at, size))
            at += size
    while at < pieces:
        groups.append((at, min(4, pieces - at)))
        at += groups[-1][1]
    return groups


def fast_kernel(digits, micro, acts, cotan, counts, weight, moment, second, packed, counts_held, acts_held, cotan_held,
                acts_out, cotan_out, acts_in, cotan_in, rhs, grad, got, state, shard, load_sem, part_send, part_recv,
                send_sem, recv_sem, up_sem):
    section = lax.axis_index("section")
    dp = lax.axis_index("dp")
    mirror = (dp, lax.axis_size("section") - 1 - section)
    planes = digits[2][0]
    strides = [stride for count, stride in digits]
    here = [lax.rem(lax.div(dp, stride), count) for count, stride in digits]
    across = [(1 - 2 * here[axis]) * strides[axis] for axis in range(2)]
    rows, depth = acts.shape[1], acts.shape[2]
    width = cotan.shape[2]
    slots = rows // micro
    pieces = lax.axis_size("dp")
    piece = depth // pieces
    per_row = width // LANES
    spans = spans_of(piece)
    tables = [send_table(z, planes, spans) for z in range(planes)]
    landings = [landing_of(z, planes, spans) for z in range(planes)]
    parts_in = part_groups(pieces)

    loads = [
        pltpu.make_async_copy(cotan, cotan_held, load_sem.at[0]),
        pltpu.make_async_copy(counts, counts_held, load_sem.at[1]),
        pltpu.make_async_copy(acts.at[1], acts_held.at[1], load_sem.at[2]),
        pltpu.make_async_copy(acts.at[0], acts_held.at[0], load_sem.at[3]),
    ]
    state_loads = [pltpu.make_async_copy(array, state.at[i], load_sem.at[4]) for i, array in enumerate((weight, moment, second))]
    for load in loads:
        load.start()

    barrier = pltpu.get_barrier_semaphore()
    pl.semaphore_signal(barrier, inc=1, device_id=mirror, device_id_type=MESH)
    for axis in range(2):
        @pl.when(here[axis] == 0)
        def greet():
            pl.semaphore_signal(barrier, inc=1, device_id=(dp + across[axis], section), device_id_type=MESH)
    for step in range(1, planes):
        @pl.when(here[2] + step < planes)
        def greet_plane():
            pl.semaphore_signal(barrier, inc=1, device_id=(dp + step * strides[2], section), device_id_type=MESH)

    def masked(k):
        parts = []
        for b in range(micro):
            block = cotan_held[k, b * slots:(b + 1) * slots, :].astype(jnp.float32)
            place = lax.broadcasted_iota(jnp.int32, (slots, width), 0)
            parts.append(jnp.where(place < counts_held[b, k], block, 0.0))
        return parts[0] if micro == 1 else jnp.concatenate(parts, axis=0)

    def to_mirror(src, dst, sent, received):
        return pltpu.make_async_remote_copy(
            src_ref=src, dst_ref=dst, send_sem=part_send.at[sent], recv_sem=part_recv.at[received],
            device_id=mirror, device_id_type=MESH)

    cotan_swap = to_mirror(cotan_out, cotan_in, 0, 0)
    group_at = {at + i: g for g, (at, size) in enumerate(parts_in) for i in range(size)}
    acts_swap = [to_mirror(acts_out.at[at], acts_in.at[at], 1, 1 + group_at[at]) for at in range(pieces)]
    loads[0].wait()
    loads[1].wait()
    cotan_out[...] = masked(1)
    pl.semaphore_wait(barrier, 1 + here[0] + here[1] + here[2])
    cotan_swap.start()
    rhs[0:rows, :] = masked(0).astype(jnp.bfloat16)
    for axis in range(2):
        @pl.when(here[axis] == 1)
        def answer():
            pl.semaphore_signal(up_sem.at[axis], inc=1, device_id=(dp + across[axis], section), device_id_type=MESH)
    for step in range(1, planes):
        @pl.when(here[2] >= step)
        def answer_plane():
            pl.semaphore_signal(up_sem.at[1 + step], inc=1, device_id=(dp - step * strides[2], section), device_id_type=MESH)
    loads[2].wait()

    def run(z):
        table = tables[z]
        places, groups, unused = landings[z]
        order = ORDERS[z]
        owners = []
        for key in order:
            if table[key][3] not in owners:
                owners.append(table[key][3])
        owners.append((0, 0, z))

        def owner_index(owner):
            return dp + owner[0] * across[0] + owner[1] * across[1] + (owner[2] - z) * strides[2]

        def columns(owner):
            return pl.ds(pl.multiple_of(owner_index(owner) * piece, LANES), piece)

        for at, owner in enumerate(owners):
            acts_out[at] = acts_held[1, :, columns(owner)].astype(jnp.float32)
            acts_swap[at].start()
        for load in state_loads:
            load.start()
        loads[3].wait()
        cotan_swap.wait_recv()
        rhs[rows:2 * rows, :] = cotan_in[...].astype(jnp.bfloat16)
        swapped = set()

        def make(at):
            g = group_at[at]
            if g not in swapped:
                swapped.add(g)
                part = acts_in.at[pl.ds(*parts_in[g])]
                to_mirror(part, part, 1, 1 + g).wait_recv()
            lhs = jnp.concatenate([acts_held[0, :, columns(owners[at])], acts_in[at].astype(jnp.bfloat16)], axis=0)
            first = pl.multiple_of(owner_index(owners[at]) * piece, piece)
            grad[pl.ds(first, piece), :] = lax.dot_general(
                lhs, rhs[...], (((0,), (0,)), ((), ())), preferred_element_type=jnp.float32)

        def block(owner, span):
            return pl.ds(pl.multiple_of(owner_index(owner) * piece + span[0], 8), span[1])

        def copy_of(key):
            axis, target, needs, owner = table[key]
            place, size, at = landings[target][0][key_there(key, z)]
            device = dp + across[axis] if axis < 2 else dp + (target - z) * strides[2]
            return pltpu.make_async_remote_copy(
                src_ref=grad.at[block(owner, span_of(key, spans)), :], dst_ref=got.at[pl.ds(place, size), :],
                send_sem=send_sem.at[0], recv_sem=recv_sem.at[at], device_id=(device, section), device_id_type=MESH)

        landed = set()

        def arrived(key, span):
            place, size, at = places[key]
            if at not in landed:
                landed.add(at)
                start = places[groups[at][0]][0]
                whole = got.at[pl.ds(start, sum(places[k][1] for k in groups[at])), :]
                pltpu.make_async_remote_copy(
                    src_ref=whole, dst_ref=whole, send_sem=send_sem.at[0], recv_sem=recv_sem.at[at],
                    device_id=mirror, device_id_type=MESH).wait_recv()
            place += span[0] - span_of(key, spans)[0]
            return got[place:place + span[1], :]

        met, done = set(), 0
        for key in order:
            axis, target, needs, owner = table[key]
            while done <= owners.index(owner):
                make(done)
                done += 1
            if needs:
                span = span_of(key, spans)
                at = block(owner, span)
                total = grad[at, :]
                for need in needs:
                    total += arrived(need, span)
                grad[at, :] = total
            if axis < 2 and axis not in met:
                met.add(axis)

                @pl.when(here[axis] == 0)
                def wait_up():
                    pl.semaphore_wait(up_sem.at[axis], 1)
            if axis == 2 and target > z and 1 + target - z not in met:
                met.add(1 + target - z)
                pl.semaphore_wait(up_sem.at[1 + target - z], 1)
            copy_of(key).start()
        for step in range(1, planes - z):
            if 1 + step not in met:
                pl.semaphore_wait(up_sem.at[1 + step], 1)
        while done < pieces:
            make(done)
            done += 1
        pltpu.make_async_copy(state, state, load_sem.at[4]).wait()
        for f, c in LASTS[z]:
            span = spans[f, c]
            total = grad[block((0, 0, z), span), :]
            for need in last_needs(f, c, z, planes):
                total += arrived(need, span)
            for part in range(per_row):
                shard[pl.ds(span[0] * per_row + part, span[1], stride=per_row), :] = total[:, part * LANES:(part + 1) * LANES]
            flat = slice(span[0] * per_row, (span[0] + span[1]) * per_row)
            updated = adamw_shard(shard[flat, :], state[0, flat, :], state[1, flat, :], state[2, flat, :])
            for i in range(3):
                packed[i, flat, :] = updated[i]
        cotan_swap.wait_send()
        to_mirror(acts_out, acts_in, 1, 1).wait_send()
        sent = grad.at[pl.ds(0, sum(span_of(key, spans)[1] for key in order)), :]
        pltpu.make_async_remote_copy(
            src_ref=sent, dst_ref=sent, send_sem=send_sem.at[0], recv_sem=recv_sem.at[0],
            device_id=mirror, device_id_type=MESH).wait_send()

    for z in range(planes):
        pl.when(here[2] == z)(functools.partial(run, z))


def put_kernel(packed, new_weight, new_moment, new_second, sem):
    copies = [pltpu.make_async_copy(packed.at[i], out, sem.at[i]) for i, out in enumerate((new_weight, new_moment, new_second))]
    for copy in copies:
        copy.start()
    for copy in copies:
        copy.wait()


def fast_fits(digits, acts, cotan, weight):
    planes, depth, width = digits[2][0], acts.shape[3], cotan.shape[3]
    piece = depth // (4 * planes)
    unit = spans_of(piece)
    whole = sum(rows for (f, c), (at, rows) in unit.items() if f in "ABZ")
    return (digits[0][0] == 2 and digits[1][0] == 2 and planes == len(ORDERS) and piece % LANES == 0 and whole == piece
            and width % LANES == 0 and piece * width == weight.shape[1])


def fast_shards(digits, acts, cotan, counts, weight, moment, second):
    micro = counts.shape[3]
    rows, depth = acts.shape[2], acts.shape[3]
    width = cotan.shape[3]
    shard_rows = weight.shape[1] // LANES
    planes = digits[2][0]
    pieces = 4 * planes
    spans = spans_of(depth // pieces)
    landings = [landing_of(z, planes, spans) for z in range(planes)]
    received = max(len(groups) for places, groups, total in landings)
    space = max(total for places, groups, total in landings)
    hbm = pl.BlockSpec(memory_space=pl.ANY)
    vmem = pl.BlockSpec(memory_space=pltpu.VMEM)
    flat = (shard_rows, LANES)
    packed = pl.pallas_call(
        functools.partial(fast_kernel, digits, micro),
        out_shape=pltpu.VMEM((3, *flat), jnp.float32),
        in_specs=[hbm] * 6,
        out_specs=vmem,
        scratch_shapes=[
            pltpu.SMEM((micro, 2), jnp.int32),
            pltpu.VMEM((2, rows, depth), jnp.bfloat16),
            pltpu.VMEM((2, rows, width), jnp.bfloat16),
            pltpu.VMEM((pieces, rows, depth // pieces), jnp.float32),
            pltpu.VMEM((rows, width), jnp.float32),
            pltpu.VMEM((pieces, rows, depth // pieces), jnp.float32),
            pltpu.VMEM((rows, width), jnp.float32),
            pltpu.VMEM((2 * rows, width), jnp.bfloat16),
            pltpu.VMEM((depth, width), jnp.float32),
            pltpu.VMEM((space, width), jnp.float32),
            pltpu.VMEM((3, *flat), jnp.float32),
            pltpu.VMEM(flat, jnp.float32),
            pltpu.SemaphoreType.DMA((5,)), pltpu.SemaphoreType.DMA((2,)), pltpu.SemaphoreType.DMA((1 + len(part_groups(pieces)),)),
            pltpu.SemaphoreType.DMA((1,)), pltpu.SemaphoreType.DMA((received,)), pltpu.SemaphoreType.REGULAR((1 + planes,)),
        ],
        compiler_params=pltpu.CompilerParams(collective_id=0, has_side_effects=True, vmem_limit_bytes=66 * 10**6),
        name="reduce_adamw",
    )(acts[0], cotan[0], counts[0, :, 0, :].T, *(array.reshape(flat) for array in (weight, moment, second)))
    outs = pl.pallas_call(
        put_kernel,
        out_shape=(jax.ShapeDtypeStruct(flat, jnp.float32),) * 3,
        in_specs=[vmem],
        out_specs=(hbm, hbm, hbm),
        scratch_shapes=[pltpu.SemaphoreType.DMA((3,))],
        name="put",
    )(pltpu.with_memory_space_constraint(packed, pltpu.VMEM))
    return tuple(array.reshape(weight.shape) for array in outs)


def solution(mesh):
    in_specs = (
        P("section", None, "dp", None),
        P("section", None, "dp", None),
        P("section", None, "dp", None),
        P("section", "dp"),
        P("section", "dp"),
        P("section", "dp"),
    )
    out_specs = (P("section", "dp"), P("section", "dp"), P("section", "dp"))
    digits = dp_digits(mesh)

    def body(acts, cotan, counts, weight, moment, second):
        form = fast_shards if fast_fits(digits, acts, cotan, weight) else shards
        return form(digits, acts, cotan, counts, weight, moment, second)

    return jax.shard_map(body, mesh=mesh, in_specs=in_specs, out_specs=out_specs, check_vma=False)
```

```python
import functools
import jax
import jax.numpy as jnp
from jax import lax
from jax.experimental import pallas as pl
from jax.experimental.pallas import tpu as pltpu
from jax.sharding import PartitionSpec as P

LANES = 128
MESH = pl.DeviceIdType.MESH


CHUNKS = (
    {"A": (7,), "B": (6,), "Z": ((1, 2),)},
    {"A": (6,), "B": (6,), "Z": ((2, 2),)},
    {"A": (6,), "B": (6,), "Z": ((2, 2),)},
    {"A": (6,), "B": (5,), "Z": ((2, 3),)},
)
RELAYS = ((3, 0), (0, 3), (3, 1))
LASTS = (
    (("C", 0), ("D", 0), ("A", 0), ("B", 0)),
    (("C", 0), ("D", 0), ("A", 0), ("B", 0)),
    (("C", 0), ("D", 0), ("A", 0), ("B", 0)),
    (("C", 0), ("D", 0), ("A", 0), ("B", 0)),
)
ORDERS = (
    (
        ("1", "A", 0, 1, 3), ("z", 0, 1, 1, 3), ("1", "B", 0, 1, 3), ("z", 0, 0, 1, 2), ("1", "A", 0, 1, 1),
        ("1", "A", 0, 0, 3), ("z", 0, 0, 1, 3), ("z", 0, 0, 0, 3), ("1", "A", 0, 1, 2), ("1", "B", 0, 1, 0), ("z", 0, 1, 0, 3),
        ("1", "B", 0, 1, 2), ("z", 0, 1, 1, 2), ("1", "B", 0, 1, 1), ("z", 0, 0, 0, 2), ("2", "B", 0, 3), ("1", "B", 0, 0, 2),
        ("2", "B", 0, 2), ("z", 0, 1, 0, 2), ("z", 0, 0, 1, 1), ("z", 0, 1, 1, 1), ("2", "A", 0, 3), ("1", "A", 0, 1, 0),
        ("z", 0, 1, 0, 1), ("1", "B", 0, 0, 3), ("2", "A", 0, 1), ("1", "A", 0, 0, 1), ("1", "A", 0, 0, 2),
        ("1", "B", 0, 0, 1), ("2", "A", 0, 2), ("2", "B", 0, 1), ("3", "A", 0, 3), ("3", "B", 0, 3), ("x", "C", 0, 1),
        ("x", "C", 0, 0), ("x", "D", 0, 1), ("1", "B", 0, 0, 0), ("2", "B", 0, 0), ("3", "B", 0, 2), ("z", 0, 0, 0, 1),
        ("1", "A", 0, 0, 0), ("2", "A", 0, 0), ("x", "D", 0, 0), ("3", "A", 0, 1), ("3", "A", 0, 2), ("y", "C", 0),
        ("3", "B", 0, 1), ("y", "D", 0),
    ),
    (
        ("1", "A", 0, 1, 2), ("1", "B", 0, 1, 2), ("1", "A", 0, 0, 2), ("1", "A", 0, 1, 0), ("1", "B", 0, 1, 3),
        ("1", "B", 0, 1, 0), ("1", "A", 0, 0, 0), ("z", 0, 1, 1, 3), ("2", "A", 0, 2), ("1", "B", 0, 0, 0), ("z", 0, 0, 1, 2),
        ("z", 0, 0, 1, 3), ("z", 0, 0, 0, 3), ("2", "B", 0, 0), ("1", "A", 0, 1, 3), ("2", "B", 0, 2), ("2", "A", 0, 0),
        ("2", "B", 0, 3), ("1", "B", 0, 0, 2), ("z", 0, 1, 1, 0), ("z", 0, 1, 0, 3), ("z", 0, 1, 1, 2), ("1", "B", 0, 0, 3),
        ("1", "B", 0, 1, 1), ("1", "A", 0, 1, 1), ("3", "A", 0, 2), ("z", 0, 0, 1, 0), ("1", "A", 0, 0, 3), ("z", 0, 0, 0, 2),
        ("z", 0, 1, 0, 2), ("z", 0, 1, 0, 0), ("3", "A", 0, 0), ("2", "A", 0, 3), ("3", "B", 0, 0), ("3", "B", 0, 2),
        ("x", "C", 0, 1), ("1", "A", 0, 0, 1), ("x", "D", 0, 0), ("x", "C", 0, 0), ("z", 0, 0, 0, 0), ("x", "D", 0, 1),
        ("2", "A", 0, 1), ("2", "B", 0, 1), ("1", "B", 0, 0, 1), ("3", "B", 0, 3), ("3", "A", 0, 3), ("y", "D", 0),
        ("y", "C", 0),
    ),
    (
        ("1", "B", 0, 0, 3), ("1", "B", 0, 1, 0), ("1", "A", 0, 1, 1), ("1", "B", 0, 1, 3), ("1", "B", 0, 1, 1),
        ("1", "A", 0, 1, 0), ("1", "B", 0, 0, 0), ("1", "B", 0, 1, 2), ("z", 0, 1, 1, 0), ("1", "A", 0, 1, 2),
        ("1", "A", 0, 1, 3), ("z", 0, 0, 1, 0), ("2", "A", 0, 0), ("1", "B", 0, 0, 1), ("2", "B", 0, 3), ("z", 0, 1, 0, 0),
        ("2", "A", 0, 1), ("1", "A", 0, 0, 0), ("z", 0, 1, 1, 3), ("z", 0, 0, 0, 0), ("z", 0, 1, 1, 1), ("2", "B", 0, 0),
        ("2", "A", 0, 3), ("z", 0, 0, 1, 1), ("2", "B", 0, 1), ("z", 0, 0, 1, 3), ("1", "A", 0, 0, 3), ("x", "D", 0, 1),
        ("x", "C", 0, 1), ("z", 0, 1, 0, 3), ("z", 0, 1, 0, 1), ("z", 0, 0, 0, 1), ("2", "A", 0, 2), ("3", "B", 0, 3),
        ("1", "A", 0, 0, 1), ("3", "A", 0, 0), ("z", 0, 0, 0, 3), ("3", "B", 0, 0), ("1", "A", 0, 0, 2), ("1", "B", 0, 0, 2),
        ("3", "B", 0, 1), ("2", "B", 0, 2), ("3", "A", 0, 3), ("x", "D", 0, 0), ("y", "D", 0), ("x", "C", 0, 0),
        ("3", "A", 0, 1), ("y", "C", 0),
    ),
    (
        ("z", 0, 1, 1, 0), ("1", "B", 0, 1, 0), ("1", "A", 0, 1, 0), ("1", "B", 0, 0, 0), ("z", 0, 1, 0, 0),
        ("1", "A", 0, 0, 0), ("z", 0, 1, 1, 1), ("1", "A", 0, 1, 1), ("z", 0, 0, 1, 0), ("z", 0, 0, 0, 1), ("1", "B", 0, 1, 1),
        ("1", "A", 0, 1, 2), ("z", 0, 1, 1, 2), ("z", 0, 0, 0, 0), ("z", 0, 0, 1, 1), ("2", "A", 0, 0), ("1", "B", 0, 1, 2),
        ("1", "B", 0, 1, 3), ("2", "B", 0, 0), ("z", 0, 1, 0, 1), ("z", 0, 1, 0, 2), ("2", "B", 0, 1), ("3", "A", 0, 0),
        ("z", 0, 0, 1, 2), ("1", "B", 0, 0, 1), ("2", "A", 0, 1), ("1", "A", 0, 0, 1), ("x", "C", 0, 1), ("1", "A", 0, 0, 2),
        ("2", "B", 0, 2), ("3", "B", 0, 0), ("2", "A", 0, 2), ("1", "B", 0, 0, 2), ("3", "B", 0, 1), ("1", "A", 0, 1, 3),
        ("1", "A", 0, 0, 3), ("3", "A", 0, 1), ("x", "D", 0, 1), ("y", "C", 0), ("x", "C", 0, 0), ("3", "A", 0, 2),
        ("1", "B", 0, 0, 3), ("2", "B", 0, 3), ("3", "B", 0, 2), ("x", "D", 0, 0), ("z", 0, 0, 0, 2), ("2", "A", 0, 3),
        ("y", "D", 0),
    ),
)


def adamw_shard(grad, weight_now, moment_now, second_now):
    new_m = 0.9 * moment_now + 0.1 * grad
    new_v = 0.95 * second_now + 0.05 * grad * grad
    corr_m = new_m / (1.0 - 0.9**10)
    corr_v = new_v / (1.0 - 0.95**10)
    new_w = weight_now - 0.01 * (corr_m / (jnp.sqrt(corr_v) + 1e-08) + 0.1 * weight_now)
    return (new_w, new_m, new_v)


def adamw_kernel(grad, weight, moment, second, new_weight, new_moment, new_second):
    new_w, new_m, new_v = adamw_shard(grad[...], weight[...], moment[...], second[...])
    new_weight[...] = new_w
    new_moment[...] = new_m
    new_second[...] = new_v


def dp_digits(mesh):
    size = mesh.shape["dp"]
    line = mesh.devices.reshape(size, -1)[:, 0]
    digits = []
    if hasattr(line[0], "coords"):
        for axis in range(3):
            at = [device.coords[axis] for device in line]
            if len(set(at)) > 1:
                digits.append((len(set(at)), next(j for j in range(size) if at[j] != at[0])))
    total = 1
    for count, stride in digits:
        total *= count
    if total != size:
        digits = [(size, 1)] if size > 1 else []
    digits.sort()
    return [(1, 1)] * (3 - len(digits)) + digits


def axis_orders(digits):
    a, b, c = digits
    return [(a, b, c), (b, a, c), (c, a, b), (c, b, a)]


def row_spans(shard_rows):
    late = shard_rows // 128 * 8
    early = (shard_rows - 2 * late) // 2
    spans = [(0, early), (early, early), (2 * early, late), (2 * early + late, late)]
    return spans[:4 if late else 2]


def reduce_kernel(digits, micro, pieces, acts, cotan, counts, out, acts_held, cotan_held, acts_out, cotan_out, acts_in, cotan_in, rhs,
                  grad, got1, got2, got3, load_sem, part_send, part_recv, send1, recv1, send2, recv2, send3, recv3):
    sections = lax.axis_size("section")
    section = lax.axis_index("section")
    dp = lax.axis_index("dp")
    mirror = sections - 1 - section

    def moved(step, digit):
        count, stride = digit
        mine = lax.rem(lax.div(dp, stride), count)
        return (lax.rem(mine + step, count) - mine) * stride

    peers = [(dp, mirror)]
    for digit in digits:
        peers += [(dp + moved(step, digit), section) for step in range(1, digit[0])]
    barrier = pltpu.get_barrier_semaphore()
    for peer in peers:
        pl.semaphore_signal(barrier, inc=1, device_id=peer, device_id_type=MESH)
    loads = [
        pltpu.make_async_copy(cotan, cotan_held, load_sem.at[0]),
        pltpu.make_async_copy(acts.at[1], acts_held.at[1], load_sem.at[1]),
        pltpu.make_async_copy(acts.at[0], acts_held.at[0], load_sem.at[2]),
    ]
    for load in loads:
        load.start()

    rows, depth = acts.shape[1], acts.shape[2]
    width = cotan.shape[2]
    slots = rows // micro
    shard_rows = out.shape[0]
    orders = axis_orders(digits)
    spans = row_spans(shard_rows)
    last = digits[2]
    per_row = width // LANES

    def masked(k):
        parts = []
        for b in range(micro):
            block = cotan_held[k, b * slots:(b + 1) * slots, :].astype(jnp.float32)
            place = lax.broadcasted_iota(jnp.int32, (slots, width), 0)
            parts.append(jnp.where(place < counts[b, k], block, 0.0))
        return parts[0] if micro == 1 else jnp.concatenate(parts, axis=0)

    steps3 = sorted(range(1, last[0]), key=lambda step: -min(step, last[0] - step)) + [0]
    piece = depth // pieces
    by_owner = pieces == lax.axis_size("dp")
    kinds = {"forward": [], "own": [], "mine": []}
    for step_a in range(digits[0][0]):
        for step_b in range(digits[1][0]):
            kind = "forward" if step_a and step_b else "own" if step_a or step_b else "mine"
            kinds[kind].append((step_a, step_b))
    groups = [("forward", 0), ("own", 0), ("forward", 1)]
    groups += [(kind, i) for i in range(len(steps3)) for kind in ("own", "forward", "mine") if (kind, i) not in groups]
    owners, places, group_of = [], [], {}
    for kind, i in groups:
        if i < len(steps3):
            group_of[kind, i] = range(len(owners), len(owners) + len(kinds[kind]))
            for step_a, step_b in kinds[kind]:
                places.append((step_a, step_b, steps3[i]))
                owners.append(dp + moved(step_a, digits[0]) + moved(step_b, digits[1]) + moved(steps3[i], last))
    if not by_owner:
        owners = list(range(pieces))

    def columns(at):
        start = owners[at] * piece
        return pl.ds(start if isinstance(start, int) else pl.multiple_of(start, LANES), piece)

    def to_mirror(src, dst, at):
        return pltpu.make_async_remote_copy(
            src_ref=src, dst_ref=dst, send_sem=part_send.at[at], recv_sem=part_recv.at[at],
            device_id=(dp, mirror), device_id_type=MESH)

    exchange = [to_mirror(acts_out.at[at], acts_in.at[at], at) for at in range(pieces)]
    exchange.append(to_mirror(cotan_out, cotan_in, pieces))
    loads[0].wait()
    cotan_out[...] = masked(1)
    rhs[0:rows, :] = masked(0).astype(jnp.bfloat16)
    loads[1].wait()
    for at in range(pieces):
        acts_out[at] = acts_held[1, :, columns(at)].astype(jnp.float32)
    pl.semaphore_wait(barrier, len(peers))
    exchange[pieces].start()
    for copy in exchange[:pieces]:
        copy.start()
    loads[2].wait()
    exchange[pieces].wait_recv()
    rhs[rows:2 * rows, :] = cotan_in[...].astype(jnp.bfloat16)

    def make(at):
        exchange[at].wait_recv()
        lhs = jnp.concatenate([acts_held[0, :, columns(at)], acts_in[at].astype(jnp.bfloat16)], axis=0)
        product = lax.dot_general(lhs, rhs[...], (((0,), (0,)), ((), ())), preferred_element_type=jnp.float32)
        first = owners[at] * (piece * per_row)
        if not isinstance(first, int):
            first = pl.multiple_of(first, 8)
        for c in range(per_row):
            grad[pl.ds(first + c, piece, stride=per_row), :] = product[:, c * LANES:(c + 1) * LANES]

    def make_group(kind, i):
        if by_owner and (kind, i) in group_of:
            for at in group_of.pop((kind, i)):
                make(at)
                made.append(places[at])

    made = []
    if not by_owner:
        for at in range(pieces):
            make(at)
        made += places

    def block(o, step1, step2, step3):
        first, second, third = orders[o]
        owner = dp + moved(step1, first) + moved(step2, second) + moved(step3, third)
        return grad.at[pl.ds(pl.multiple_of(owner * shard_rows + spans[o][0], 8), spans[o][1]), :]

    def base1(o, step1, step2, step3):
        first, second, third = orders[o]
        return ((step1 - 1) * second[0] + step2) * third[0] + step3

    def stage1(o, step1, step2, step3):
        at = base1(o, step1, step2, step3)
        return pltpu.make_async_remote_copy(
            src_ref=block(o, step1, step2, step3), dst_ref=got1[o].at[at], send_sem=send1[o].at[at], recv_sem=recv1[o].at[at],
            device_id=(dp + moved(step1, orders[o][0]), section), device_id_type=MESH)

    def stage2(o, step2, step3):
        at = (step2 - 1) * orders[o][2][0] + step3
        return pltpu.make_async_remote_copy(
            src_ref=block(o, 0, step2, step3), dst_ref=got2[o].at[at], send_sem=send2[o].at[at], recv_sem=recv2[o].at[at],
            device_id=(dp + moved(step2, orders[o][1]), section), device_id_type=MESH)

    def stage3(o, step3):
        at = step3 - 1
        return pltpu.make_async_remote_copy(
            src_ref=block(o, 0, 0, step3), dst_ref=got3[o].at[at], send_sem=send3[o].at[at], recv_sem=recv3[o].at[at],
            device_id=(dp + moved(step3, orders[o][2]), section), device_id_type=MESH)

    started = []

    def start(copy):
        copy.start()
        started.append(copy)

    def arrived1(o, step2, step3):
        total = block(o, 0, step2, step3)[...]
        for step1 in range(1, orders[o][0][0]):
            stage1(o, step1, step2, step3).wait_recv()
            total += got1[o][base1(o, step1, step2, step3)]
        return total

    def arrived2(o, step3):
        total = arrived1(o, 0, step3)
        for step2 in range(1, orders[o][1][0]):
            stage2(o, step2, step3).wait_recv()
            total += got2[o][(step2 - 1) * orders[o][2][0] + step3]
        return total

    def send_forward(i):
        if i < len(steps3):
            for o in range(2):
                for step1 in range(1, orders[o][0][0]):
                    for step2 in range(1, orders[o][1][0]):
                        start(stage1(o, step1, step2, steps3[i]))

    def send_own(i):
        if i < len(steps3):
            for o in range(2):
                for step1 in range(1, orders[o][0][0]):
                    start(stage1(o, step1, 0, steps3[i]))

    def send_second(i):
        for o in range(2):
            for step2 in range(1, orders[o][1][0]):
                block(o, 0, step2, steps3[i])[...] = arrived1(o, step2, steps3[i])
                start(stage2(o, step2, steps3[i]))

    def send_third(i):
        for o in range(2):
            block(o, 0, 0, steps3[i])[...] = arrived2(o, steps3[i])
            start(stage3(o, steps3[i]))

    late = range(2, len(spans))

    def late_first(step2, step3, step1):
        for o in late:
            if step1:
                start(stage1(o, step1, *((step2, step3) if orders[o][1] is digits[0] else (step3, step2))))

    def late_second():
        for o in late:
            for step2 in range(1, orders[o][1][0]):
                for step3 in reversed(range(orders[o][2][0])):
                    block(o, 0, step2, step3)[...] = arrived1(o, step2, step3)
                    start(stage2(o, step2, step3))

    def late_third():
        for o in late:
            for step3 in range(1, orders[o][2][0]):
                block(o, 0, 0, step3)[...] = arrived2(o, step3)
                start(stage3(o, step3))

    def send_late():
        while made:
            late_first(*made.pop(0))

    end = len(steps3) - 1
    make_group("forward", 0)
    send_forward(0)
    make_group("own", 0)
    send_own(0)
    send_late()
    make_group("forward", 1)
    if end > 1:
        send_forward(1)
    send_late()
    for kind, i in list(group_of):
        make_group(kind, i)
        send_late()
    for i in range(end + 1):
        if i == end and i:
            send_third(i - 1)
        send_second(i)
        if i == end - 1:
            send_forward(end)
        send_own(i + 1)
        if i + 2 < end:
            send_forward(i + 2)
        if 1 <= i < end:
            send_third(i - 1)
        if i == end - 2:
            late_second()
        if i == end - 1:
            late_third()
    if len(steps3) < 3:
        late_second()
    if len(steps3) < 2:
        late_third()
    for o in reversed(range(len(spans))):
        total = arrived2(o, 0)
        for step3 in range(1, orders[o][2][0]):
            stage3(o, step3).wait_recv()
            total += got3[o][step3 - 1]
        out[spans[o][0]:spans[o][0] + spans[o][1], :] = total
    for copy in exchange + started:
        copy.wait_send()


def shards(digits, acts, cotan, counts, weight, moment, second):
    micro = counts.shape[3]
    rows, depth = acts.shape[2], acts.shape[3]
    width = cotan.shape[3]
    shard_rows = weight.shape[1] // LANES
    piece = weight.shape[1] // width
    pieces = depth // piece if piece % LANES == 0 and weight.shape[1] % width == 0 else depth // (2 * LANES)
    orders = axis_orders(digits)
    spans = row_spans(shard_rows)
    orders = orders[:len(spans)]
    counts1 = [(first[0] - 1) * second[0] * third[0] for first, second, third in orders]
    counts2 = [(second[0] - 1) * third[0] for first, second, third in orders]
    counts3 = [third[0] - 1 for first, second, third in orders]

    def buffers(sizes):
        return [pltpu.VMEM((max(size, 1), span[1], LANES), jnp.float32) for size, span in zip(sizes, spans)]

    def semaphores(sizes):
        return [pltpu.SemaphoreType.DMA((max(size, 1),)) for size in sizes]

    hbm = pl.BlockSpec(memory_space=pl.ANY)
    vmem = pl.BlockSpec(memory_space=pltpu.VMEM)
    shard = pl.pallas_call(
        functools.partial(reduce_kernel, digits, micro, pieces),
        out_shape=jax.ShapeDtypeStruct((shard_rows, LANES), jnp.float32),
        in_specs=[hbm, hbm, pl.BlockSpec(memory_space=pltpu.SMEM)],
        out_specs=vmem,
        scratch_shapes=[
            pltpu.VMEM((2, rows, depth), jnp.bfloat16),
            pltpu.VMEM((2, rows, width), jnp.bfloat16),
            pltpu.VMEM((pieces, rows, depth // pieces), jnp.float32),
            pltpu.VMEM((rows, width), jnp.float32),
            pltpu.VMEM((pieces, rows, depth // pieces), jnp.float32),
            pltpu.VMEM((rows, width), jnp.float32),
            pltpu.VMEM((2 * rows, width), jnp.bfloat16),
            pltpu.VMEM((depth * width // LANES, LANES), jnp.float32),
            buffers(counts1), buffers(counts2), buffers(counts3),
            pltpu.SemaphoreType.DMA((3,)), pltpu.SemaphoreType.DMA((pieces + 1,)), pltpu.SemaphoreType.DMA((pieces + 1,)),
            semaphores(counts1), semaphores(counts1), semaphores(counts2), semaphores(counts2),
            semaphores(counts3), semaphores(counts3),
        ],
        compiler_params=pltpu.CompilerParams(collective_id=0, has_side_effects=True),
        name="reduce_grad",
    )(acts[0], cotan[0], counts[0, :, 0, :].T)
    flat = jax.ShapeDtypeStruct((shard_rows, LANES), jnp.float32)
    outs = pl.pallas_call(
        adamw_kernel,
        out_shape=(flat, flat, flat),
        in_specs=[vmem] * 4,
        out_specs=(vmem, vmem, vmem),
        name="adamw",
    )(shard, *(array.reshape(shard_rows, LANES) for array in (weight, moment, second)))
    return tuple(array.reshape(weight.shape) for array in outs)


AXES = {"A": (0, 1), "B": (1, 0), "C": (0, 1), "D": (1, 0)}


def flipped(family, first, second):
    return (first, second) if AXES[family][0] == 0 else (second, first)


def planes_beside(z, planes):
    return [p for p in (z - 1, z + 1) if 0 <= p < planes]


def crossed(c, place, z, planes):
    return tuple(("z", c, *place, z, p) for p in planes_beside(z, planes))


def toward(z, k):
    return 1 if k > z else -1


def third_needs(f, c, k, z):
    before = z - toward(z, k)
    return (("1", f, c, 0, k), ("2", f, c, k)) + ((("r", f, c, k, before),) if (before, k) in RELAYS else ())


def send_table(z, planes, spans):
    table = {}
    for f, c in spans[z]:
        if f in AXES:
            first, second = AXES[f]
        if f in "AB":
            for k in range(planes):
                for b in range(2):
                    table["1", f, c, b, k] = (first, z, (), flipped(f, 1, b) + (k,))
                table["2", f, c, k] = (second, z, (("1", f, c, 1, k),), flipped(f, 0, 1) + (k,))
                if k != z:
                    target = z + toward(z, k) if (z, k) in RELAYS else k
                    table["3", f, c, k] = (2, target, third_needs(f, c, k, z), (0, 0, k))
        elif f in "CD":
            for b in range(2):
                place = flipped(f, 1, b)
                table["x", f, c, b] = (first, z, crossed(c, place, z, planes), place + (z,))
            place = flipped(f, 0, 1)
            table["y", f, c] = (second, z, crossed(c, place, z, planes) + (("x", f, c, 1),), place + (z,))
        else:
            for k in range(planes):
                before = z - toward(z, k)
                for a in range(2 if k != z else 0):
                    for b in range(2):
                        needs = (("z", c, a, b, k, before),) if 0 <= before < planes else ()
                        table["z", c, a, b, k] = (2, z + toward(z, k), needs, (a, b, k))
    return table


def last_needs(f, c, z, planes):
    if f in "AB":
        return (("1", f, c, 0, z), ("2", f, c, z)) + tuple(("3", f, c, p) for p in range(planes) if p != z and (p, z) not in RELAYS)
    return crossed(c, (0, 0), z, planes) + (("x", f, c, 0), ("y", f, c))


def wait_groups(z, planes, spans):
    groups = []
    for f, c in spans[z]:
        if f in "AB":
            for k in range(planes):
                groups.append((("1", f, c, 1, k),))
                groups.append(third_needs(f, c, k, z) if k != z else last_needs(f, c, z, planes))
        elif f in "CD":
            groups += [(("x", f, c, 1),), (("x", f, c, 0), ("y", f, c))]
        else:
            for place in ((0, 0), (0, 1), (1, 0), (1, 1)):
                groups.append(crossed(c, place, z, planes))
                for k in range(planes):
                    before = z - toward(z, k)
                    if k != z and 0 <= before < planes:
                        groups.append((("z", c, *place, k, before),))
    return groups


def key_there(key, z):
    if key[0] == "3":
        return ("r",) + key[1:] + (z,) if (z, key[3]) in RELAYS else key[:-1] + (z,)
    return key + (z,) if key[0] == "z" else key


def span_of(key, spans, z, coming):
    if key[0] in "xy" or key[0] == "3" and coming:
        k = z
    else:
        k = key[4 if key[0] in "1z" else 3]
    return spans[k][("Z", key[1]) if key[0] == "z" else key[1:3]]


def spans_of(piece):
    planes = []
    for chunks in CHUNKS:
        total = sum(chunks["A"]) + sum(chunks["B"]) + sum(sum(pair) for pair in chunks["Z"])
        unit = piece // 8 // total * 8
        spans, at = {}, 0
        for f in "AB":
            for c, size in enumerate(chunks[f]):
                spans[f, c] = (at, size * unit)
                at += size * unit
        for c, (first, second) in enumerate(chunks["Z"]):
            spans["Z", c] = (at, (first + second) * unit)
            spans["C", c] = (at, first * unit)
            spans["D", c] = (at + first * unit, second * unit)
            at += (first + second) * unit
        planes.append(spans)
    return planes


def landing_of(z, planes, spans):
    places, at, groups = {}, 0, wait_groups(z, planes, spans)
    for i, group in enumerate(groups):
        for key in group:
            rows = span_of(key, spans, z, True)[1]
            places[key] = (at, rows, i)
            at += rows
    return places, groups, at


def part_groups(pieces):
    groups, at = [], 0
    for size in (1, 1, 1, 1, 2, 2):
        if at + size <= pieces:
            groups.append((at, size))
            at += size
    while at < pieces:
        groups.append((at, min(4, pieces - at)))
        at += groups[-1][1]
    return groups


def fast_kernel(digits, micro, acts, cotan, counts, weight, moment, second, packed, counts_held, acts_held, cotan_held,
                acts_out, cotan_out, acts_in, cotan_in, rhs, grad, got, state, shard, load_sem, part_send, part_recv,
                send_sem, recv_sem, up_sem):
    section = lax.axis_index("section")
    dp = lax.axis_index("dp")
    mirror = (dp, lax.axis_size("section") - 1 - section)
    planes = digits[2][0]
    strides = [stride for count, stride in digits]
    here = [lax.rem(lax.div(dp, stride), count) for count, stride in digits]
    across = [(1 - 2 * here[axis]) * strides[axis] for axis in range(2)]
    rows, depth = acts.shape[1], acts.shape[2]
    width = cotan.shape[2]
    slots = rows // micro
    pieces = lax.axis_size("dp")
    piece = depth // pieces
    per_row = width // LANES
    spans = spans_of(piece)
    tables = [send_table(z, planes, spans) for z in range(planes)]
    landings = [landing_of(z, planes, spans) for z in range(planes)]
    parts_in = part_groups(pieces)

    loads = [
        pltpu.make_async_copy(cotan, cotan_held, load_sem.at[0]),
        pltpu.make_async_copy(counts, counts_held, load_sem.at[1]),
        pltpu.make_async_copy(acts.at[1], acts_held.at[1], load_sem.at[2]),
        pltpu.make_async_copy(acts.at[0], acts_held.at[0], load_sem.at[3]),
    ]
    state_loads = [pltpu.make_async_copy(array, state.at[i], load_sem.at[4]) for i, array in enumerate((weight, moment, second))]
    for load in loads:
        load.start()

    barrier = pltpu.get_barrier_semaphore()
    pl.semaphore_signal(barrier, inc=1, device_id=mirror, device_id_type=MESH)
    for axis in range(2):
        @pl.when(here[axis] == 0)
        def greet():
            pl.semaphore_signal(barrier, inc=1, device_id=(dp + across[axis], section), device_id_type=MESH)
    for step in range(1, planes):
        @pl.when(here[2] + step < planes)
        def greet_plane():
            pl.semaphore_signal(barrier, inc=1, device_id=(dp + step * strides[2], section), device_id_type=MESH)

    def masked(k):
        parts = []
        for b in range(micro):
            block = cotan_held[k, b * slots:(b + 1) * slots, :].astype(jnp.float32)
            place = lax.broadcasted_iota(jnp.int32, (slots, width), 0)
            parts.append(jnp.where(place < counts_held[b, k], block, 0.0))
        return parts[0] if micro == 1 else jnp.concatenate(parts, axis=0)

    def to_mirror(src, dst, sent, received):
        return pltpu.make_async_remote_copy(
            src_ref=src, dst_ref=dst, send_sem=part_send.at[sent], recv_sem=part_recv.at[received],
            device_id=mirror, device_id_type=MESH)

    cotan_swap = to_mirror(cotan_out, cotan_in, 0, 0)
    group_at = {at + i: g for g, (at, size) in enumerate(parts_in) for i in range(size)}
    acts_swap = [to_mirror(acts_out.at[at], acts_in.at[at], 1, 1 + group_at[at]) for at in range(pieces)]
    loads[0].wait()
    loads[1].wait()
    cotan_out[...] = masked(1)
    pl.semaphore_wait(barrier, 1 + here[0] + here[1] + here[2])
    cotan_swap.start()
    rhs[0:rows, :] = masked(0).astype(jnp.bfloat16)
    for axis in range(2):
        @pl.when(here[axis] == 1)
        def answer():
            pl.semaphore_signal(up_sem.at[axis], inc=1, device_id=(dp + across[axis], section), device_id_type=MESH)
    for step in range(1, planes):
        @pl.when(here[2] >= step)
        def answer_plane():
            pl.semaphore_signal(up_sem.at[1 + step], inc=1, device_id=(dp - step * strides[2], section), device_id_type=MESH)
    loads[2].wait()

    def run(z):
        table = tables[z]
        places, groups, unused = landings[z]
        order = ORDERS[z]
        owners = []
        for key in order:
            if table[key][3] not in owners:
                owners.append(table[key][3])
        owners.append((0, 0, z))

        def owner_index(owner):
            return dp + owner[0] * across[0] + owner[1] * across[1] + (owner[2] - z) * strides[2]

        def columns(owner):
            return pl.ds(pl.multiple_of(owner_index(owner) * piece, LANES), piece)

        for at, owner in enumerate(owners):
            acts_out[at] = acts_held[1, :, columns(owner)].astype(jnp.float32)
            acts_swap[at].start()
        for load in state_loads:
            load.start()
        loads[3].wait()
        cotan_swap.wait_recv()
        rhs[rows:2 * rows, :] = cotan_in[...].astype(jnp.bfloat16)
        swapped = set()

        def make(at):
            g = group_at[at]
            if g not in swapped:
                swapped.add(g)
                part = acts_in.at[pl.ds(*parts_in[g])]
                to_mirror(part, part, 1, 1 + g).wait_recv()
            lhs = jnp.concatenate([acts_held[0, :, columns(owners[at])], acts_in[at].astype(jnp.bfloat16)], axis=0)
            first = pl.multiple_of(owner_index(owners[at]) * piece, piece)
            grad[pl.ds(first, piece), :] = lax.dot_general(
                lhs, rhs[...], (((0,), (0,)), ((), ())), preferred_element_type=jnp.float32)

        def block(owner, span):
            return pl.ds(pl.multiple_of(owner_index(owner) * piece + span[0], 8), span[1])

        def copy_of(key):
            axis, target, needs, owner = table[key]
            place, size, at = landings[target][0][key_there(key, z)]
            device = dp + across[axis] if axis < 2 else dp + (target - z) * strides[2]
            return pltpu.make_async_remote_copy(
                src_ref=grad.at[block(owner, span_of(key, spans, z, False)), :], dst_ref=got.at[pl.ds(place, size), :],
                send_sem=send_sem.at[0], recv_sem=recv_sem.at[at], device_id=(device, section), device_id_type=MESH)

        landed = set()

        def arrived(key, span):
            place, size, at = places[key]
            if at not in landed:
                landed.add(at)
                start = places[groups[at][0]][0]
                whole = got.at[pl.ds(start, sum(places[k][1] for k in groups[at])), :]
                pltpu.make_async_remote_copy(
                    src_ref=whole, dst_ref=whole, send_sem=send_sem.at[0], recv_sem=recv_sem.at[at],
                    device_id=mirror, device_id_type=MESH).wait_recv()
            place += span[0] - span_of(key, spans, z, True)[0]
            return got[place:place + span[1], :]

        met, done = set(), 0
        for key in order:
            axis, target, needs, owner = table[key]
            while done <= owners.index(owner):
                make(done)
                done += 1
            if needs:
                span = span_of(key, spans, z, False)
                at = block(owner, span)
                total = grad[at, :]
                for need in needs:
                    total += arrived(need, span)
                grad[at, :] = total
            if axis < 2 and axis not in met:
                met.add(axis)

                @pl.when(here[axis] == 0)
                def wait_up():
                    pl.semaphore_wait(up_sem.at[axis], 1)
            if axis == 2 and target > z and 1 + target - z not in met:
                met.add(1 + target - z)
                pl.semaphore_wait(up_sem.at[1 + target - z], 1)
            copy_of(key).start()
        for step in range(1, planes - z):
            if 1 + step not in met:
                pl.semaphore_wait(up_sem.at[1 + step], 1)
        while done < pieces:
            make(done)
            done += 1
        pltpu.make_async_copy(state, state, load_sem.at[4]).wait()
        for f, c in LASTS[z]:
            span = spans[z][f, c]
            total = grad[block((0, 0, z), span), :]
            for need in last_needs(f, c, z, planes):
                total += arrived(need, span)
            for part in range(per_row):
                shard[pl.ds(span[0] * per_row + part, span[1], stride=per_row), :] = total[:, part * LANES:(part + 1) * LANES]
            flat = slice(span[0] * per_row, (span[0] + span[1]) * per_row)
            updated = adamw_shard(shard[flat, :], state[0, flat, :], state[1, flat, :], state[2, flat, :])
            for i in range(3):
                packed[i, flat, :] = updated[i]
        cotan_swap.wait_send()
        to_mirror(acts_out, acts_in, 1, 1).wait_send()
        sent = grad.at[pl.ds(0, sum(span_of(key, spans, z, False)[1] for key in order)), :]
        pltpu.make_async_remote_copy(
            src_ref=sent, dst_ref=sent, send_sem=send_sem.at[0], recv_sem=recv_sem.at[0],
            device_id=mirror, device_id_type=MESH).wait_send()

    for z in range(planes):
        pl.when(here[2] == z)(functools.partial(run, z))


def put_kernel(packed, new_weight, new_moment, new_second, sem):
    copies = [pltpu.make_async_copy(packed.at[i], out, sem.at[i]) for i, out in enumerate((new_weight, new_moment, new_second))]
    for copy in copies:
        copy.start()
    for copy in copies:
        copy.wait()


def fast_fits(digits, acts, cotan, weight):
    planes, depth, width = digits[2][0], acts.shape[3], cotan.shape[3]
    piece = depth // (4 * planes)
    whole = all(sum(rows for (f, c), (at, rows) in spans.items() if f in "ABZ") == piece for spans in spans_of(piece))
    return (digits[0][0] == 2 and digits[1][0] == 2 and planes == len(ORDERS) and piece % LANES == 0 and whole
            and width % LANES == 0 and piece * width == weight.shape[1])


def fast_shards(digits, acts, cotan, counts, weight, moment, second):
    micro = counts.shape[3]
    rows, depth = acts.shape[2], acts.shape[3]
    width = cotan.shape[3]
    shard_rows = weight.shape[1] // LANES
    planes = digits[2][0]
    pieces = 4 * planes
    spans = spans_of(depth // pieces)
    landings = [landing_of(z, planes, spans) for z in range(planes)]
    received = max(len(groups) for places, groups, total in landings)
    space = max(total for places, groups, total in landings)
    hbm = pl.BlockSpec(memory_space=pl.ANY)
    vmem = pl.BlockSpec(memory_space=pltpu.VMEM)
    flat = (shard_rows, LANES)
    packed = pl.pallas_call(
        functools.partial(fast_kernel, digits, micro),
        out_shape=pltpu.VMEM((3, *flat), jnp.float32),
        in_specs=[hbm] * 6,
        out_specs=vmem,
        scratch_shapes=[
            pltpu.SMEM((micro, 2), jnp.int32),
            pltpu.VMEM((2, rows, depth), jnp.bfloat16),
            pltpu.VMEM((2, rows, width), jnp.bfloat16),
            pltpu.VMEM((pieces, rows, depth // pieces), jnp.float32),
            pltpu.VMEM((rows, width), jnp.float32),
            pltpu.VMEM((pieces, rows, depth // pieces), jnp.float32),
            pltpu.VMEM((rows, width), jnp.float32),
            pltpu.VMEM((2 * rows, width), jnp.bfloat16),
            pltpu.VMEM((depth, width), jnp.float32),
            pltpu.VMEM((space, width), jnp.float32),
            pltpu.VMEM((3, *flat), jnp.float32),
            pltpu.VMEM(flat, jnp.float32),
            pltpu.SemaphoreType.DMA((5,)), pltpu.SemaphoreType.DMA((2,)), pltpu.SemaphoreType.DMA((1 + len(part_groups(pieces)),)),
            pltpu.SemaphoreType.DMA((1,)), pltpu.SemaphoreType.DMA((received,)), pltpu.SemaphoreType.REGULAR((1 + planes,)),
        ],
        compiler_params=pltpu.CompilerParams(collective_id=0, has_side_effects=True, vmem_limit_bytes=66 * 10**6),
        name="reduce_adamw",
    )(acts[0], cotan[0], counts[0, :, 0, :].T, *(array.reshape(flat) for array in (weight, moment, second)))
    outs = pl.pallas_call(
        put_kernel,
        out_shape=(jax.ShapeDtypeStruct(flat, jnp.float32),) * 3,
        in_specs=[vmem],
        out_specs=(hbm, hbm, hbm),
        scratch_shapes=[pltpu.SemaphoreType.DMA((3,))],
        name="put",
    )(pltpu.with_memory_space_constraint(packed, pltpu.VMEM))
    return tuple(array.reshape(weight.shape) for array in outs)


def solution(mesh):
    in_specs = (
        P("section", None, "dp", None),
        P("section", None, "dp", None),
        P("section", None, "dp", None),
        P("section", "dp"),
        P("section", "dp"),
        P("section", "dp"),
    )
    out_specs = (P("section", "dp"), P("section", "dp"), P("section", "dp"))
    digits = dp_digits(mesh)

    def body(acts, cotan, counts, weight, moment, second):
        form = fast_shards if fast_fits(digits, acts, cotan, weight) else shards
        return form(digits, acts, cotan, counts, weight, moment, second)

    return jax.shard_map(body, mesh=mesh, in_specs=in_specs, out_specs=out_specs, check_vma=False)
```

```python
import functools
import jax
import jax.numpy as jnp
from jax import lax
from jax.experimental import pallas as pl
from jax.experimental.pallas import tpu as pltpu
from jax.sharding import PartitionSpec as P

LANES = 128
MESH = pl.DeviceIdType.MESH


CHUNKS = (
    {"A": (7,), "B": (6,), "Z": ((1, 2),)},
    {"A": (6,), "B": (6,), "Z": ((2, 2),)},
    {"A": (6,), "B": (6,), "Z": ((2, 2),)},
    {"A": (6,), "B": (5,), "Z": ((2, 3),)},
)
RELAYS = ((3, 1), (3, 0), (0, 2), (0, 3))
LASTS = (
    (("A", 0), ("C", 0), ("B", 0), ("D", 0)),
    (("D", 0), ("C", 0), ("B", 0), ("A", 0)),
    (("A", 0), ("C", 0), ("D", 0), ("B", 0)),
    (("D", 0), ("A", 0), ("C", 0), ("B", 0)),
)
ORDERS = (
    (
        ("1", "A", 0, 1, 2), ("z", 0, 1, 1, 2), ("1", "B", 0, 1, 2), ("1", "A", 0, 1, 3), ("z", 0, 1, 0, 3),
        ("1", "B", 0, 1, 3), ("1", "A", 0, 1, 1), ("z", 0, 1, 1, 3), ("z", 0, 0, 0, 2), ("1", "A", 0, 0, 3), ("z", 0, 0, 1, 3),
        ("1", "B", 0, 0, 3), ("1", "B", 0, 1, 1), ("1", "B", 0, 0, 1), ("1", "A", 0, 0, 2), ("z", 0, 1, 0, 2),
        ("2", "A", 0, 3), ("z", 0, 0, 0, 3), ("2", "B", 0, 3), ("2", "A", 0, 2), ("1", "A", 0, 1, 0), ("2", "B", 0, 2),
        ("z", 0, 0, 1, 2), ("z", 0, 1, 0, 1), ("z", 0, 0, 1, 1), ("z", 0, 1, 1, 1), ("1", "B", 0, 1, 0), ("1", "B", 0, 0, 2),
        ("x", "D", 0, 1), ("x", "C", 0, 1), ("3", "A", 0, 3), ("2", "B", 0, 1), ("1", "A", 0, 0, 0), ("3", "B", 0, 3),
        ("x", "C", 0, 0), ("2", "A", 0, 1), ("1", "A", 0, 0, 1), ("2", "B", 0, 0), ("2", "A", 0, 0), ("3", "A", 0, 2),
        ("3", "B", 0, 2), ("3", "B", 0, 1), ("y", "C", 0), ("y", "D", 0), ("x", "D", 0, 0), ("1", "B", 0, 0, 0),
        ("z", 0, 0, 0, 1), ("3", "A", 0, 1),
    ),
    (
        ("1", "B", 0, 1, 3), ("1", "A", 0, 1, 3), ("1", "A", 0, 1, 0), ("1", "B", 0, 1, 0), ("1", "A", 0, 0, 0),
        ("1", "B", 0, 1, 2), ("1", "B", 0, 1, 1), ("z", 0, 1, 1, 2), ("z", 0, 1, 1, 3), ("1", "B", 0, 0, 0), ("2", "B", 0, 0),
        ("1", "A", 0, 1, 2), ("z", 0, 0, 0, 2), ("z", 0, 1, 0, 3), ("2", "B", 0, 2), ("z", 0, 1, 1, 0), ("2", "A", 0, 0),
        ("2", "A", 0, 3), ("z", 0, 0, 1, 3), ("1", "A", 0, 0, 3), ("z", 0, 1, 0, 0), ("z", 0, 0, 0, 3), ("2", "B", 0, 3),
        ("z", 0, 1, 0, 2), ("1", "B", 0, 0, 3), ("3", "B", 0, 0), ("1", "A", 0, 0, 2), ("2", "A", 0, 2), ("1", "A", 0, 1, 1),
        ("z", 0, 0, 1, 2), ("3", "A", 0, 0), ("z", 0, 0, 1, 0), ("1", "B", 0, 0, 2), ("3", "A", 0, 3), ("x", "D", 0, 1),
        ("x", "C", 0, 1), ("1", "A", 0, 0, 1), ("z", 0, 0, 0, 0), ("x", "D", 0, 0), ("3", "B", 0, 3), ("1", "B", 0, 0, 1),
        ("x", "C", 0, 0), ("3", "A", 0, 2), ("2", "B", 0, 1), ("2", "A", 0, 1), ("y", "D", 0), ("y", "C", 0), ("3", "B", 0, 2),
    ),
    (
        ("1", "A", 0, 1, 2), ("1", "B", 0, 1, 0), ("1", "A", 0, 1, 0), ("1", "B", 0, 1, 1), ("1", "A", 0, 1, 3),
        ("1", "A", 0, 0, 0), ("1", "B", 0, 0, 3), ("1", "A", 0, 1, 1), ("2", "B", 0, 0), ("1", "B", 0, 1, 2),
        ("z", 0, 1, 1, 0), ("1", "B", 0, 1, 3), ("1", "A", 0, 0, 1), ("2", "B", 0, 1), ("z", 0, 1, 0, 0), ("z", 0, 0, 0, 1),
        ("2", "A", 0, 3), ("x", "D", 0, 1), ("2", "A", 0, 0), ("z", 0, 1, 1, 3), ("z", 0, 1, 0, 1), ("z", 0, 0, 1, 0),
        ("z", 0, 1, 0, 3), ("1", "B", 0, 0, 0), ("2", "B", 0, 3), ("2", "A", 0, 1), ("1", "A", 0, 0, 3), ("z", 0, 0, 1, 1),
        ("z", 0, 1, 1, 1), ("z", 0, 0, 0, 0), ("z", 0, 0, 1, 3), ("z", 0, 0, 0, 3), ("x", "C", 0, 1), ("1", "B", 0, 0, 1),
        ("2", "B", 0, 2), ("1", "B", 0, 0, 2), ("1", "A", 0, 0, 2), ("3", "A", 0, 0), ("x", "D", 0, 0), ("3", "B", 0, 0),
        ("3", "B", 0, 3), ("x", "C", 0, 0), ("2", "A", 0, 2), ("3", "A", 0, 1), ("3", "B", 0, 1), ("3", "A", 0, 3),
        ("y", "C", 0), ("y", "D", 0),
    ),
    (
        ("z", 0, 1, 1, 0), ("1", "B", 0, 1, 0), ("1", "A", 0, 1, 0), ("1", "B", 0, 0, 1), ("z", 0, 1, 0, 0),
        ("1", "A", 0, 1, 1), ("z", 0, 0, 0, 1), ("z", 0, 0, 1, 0), ("1", "A", 0, 0, 0), ("z", 0, 1, 1, 2), ("1", "B", 0, 1, 1),
        ("z", 0, 1, 0, 1), ("z", 0, 0, 1, 1), ("2", "A", 0, 0), ("z", 0, 0, 1, 2), ("2", "B", 0, 0), ("1", "A", 0, 0, 1),
        ("z", 0, 1, 1, 1), ("1", "A", 0, 1, 2), ("1", "B", 0, 0, 0), ("2", "A", 0, 1), ("z", 0, 0, 0, 0), ("2", "B", 0, 1),
        ("1", "A", 0, 1, 3), ("1", "B", 0, 1, 2), ("1", "A", 0, 0, 2), ("3", "A", 0, 0), ("1", "B", 0, 0, 2), ("3", "B", 0, 0),
        ("z", 0, 1, 0, 2), ("3", "A", 0, 1), ("2", "A", 0, 2), ("2", "B", 0, 2), ("x", "D", 0, 1), ("3", "B", 0, 1),
        ("x", "C", 0, 1), ("1", "B", 0, 1, 3), ("1", "A", 0, 0, 3), ("2", "A", 0, 3), ("z", 0, 0, 0, 2), ("3", "A", 0, 2),
        ("y", "D", 0), ("1", "B", 0, 0, 3), ("3", "B", 0, 2), ("x", "C", 0, 0), ("x", "D", 0, 0), ("2", "B", 0, 3),
        ("y", "C", 0),
    ),
)


def adamw_shard(grad, weight_now, moment_now, second_now):
    new_m = 0.9 * moment_now + 0.1 * grad
    new_v = 0.95 * second_now + 0.05 * grad * grad
    corr_m = new_m / (1.0 - 0.9**10)
    corr_v = new_v / (1.0 - 0.95**10)
    new_w = weight_now - 0.01 * (corr_m / (jnp.sqrt(corr_v) + 1e-08) + 0.1 * weight_now)
    return (new_w, new_m, new_v)


def adamw_kernel(grad, weight, moment, second, new_weight, new_moment, new_second):
    new_w, new_m, new_v = adamw_shard(grad[...], weight[...], moment[...], second[...])
    new_weight[...] = new_w
    new_moment[...] = new_m
    new_second[...] = new_v


def dp_digits(mesh):
    size = mesh.shape["dp"]
    line = mesh.devices.reshape(size, -1)[:, 0]
    digits = []
    if hasattr(line[0], "coords"):
        for axis in range(3):
            at = [device.coords[axis] for device in line]
            if len(set(at)) > 1:
                digits.append((len(set(at)), next(j for j in range(size) if at[j] != at[0])))
    total = 1
    for count, stride in digits:
        total *= count
    if total != size:
        digits = [(size, 1)] if size > 1 else []
    digits.sort()
    return [(1, 1)] * (3 - len(digits)) + digits


def axis_orders(digits):
    a, b, c = digits
    return [(a, b, c), (b, a, c), (c, a, b), (c, b, a)]


def row_spans(shard_rows):
    late = shard_rows // 128 * 8
    early = (shard_rows - 2 * late) // 2
    spans = [(0, early), (early, early), (2 * early, late), (2 * early + late, late)]
    return spans[:4 if late else 2]


def reduce_kernel(digits, micro, pieces, acts, cotan, counts, out, acts_held, cotan_held, acts_out, cotan_out, acts_in, cotan_in, rhs,
                  grad, got1, got2, got3, load_sem, part_send, part_recv, send1, recv1, send2, recv2, send3, recv3):
    sections = lax.axis_size("section")
    section = lax.axis_index("section")
    dp = lax.axis_index("dp")
    mirror = sections - 1 - section

    def moved(step, digit):
        count, stride = digit
        mine = lax.rem(lax.div(dp, stride), count)
        return (lax.rem(mine + step, count) - mine) * stride

    peers = [(dp, mirror)]
    for digit in digits:
        peers += [(dp + moved(step, digit), section) for step in range(1, digit[0])]
    barrier = pltpu.get_barrier_semaphore()
    for peer in peers:
        pl.semaphore_signal(barrier, inc=1, device_id=peer, device_id_type=MESH)
    loads = [
        pltpu.make_async_copy(cotan, cotan_held, load_sem.at[0]),
        pltpu.make_async_copy(acts.at[1], acts_held.at[1], load_sem.at[1]),
        pltpu.make_async_copy(acts.at[0], acts_held.at[0], load_sem.at[2]),
    ]
    for load in loads:
        load.start()

    rows, depth = acts.shape[1], acts.shape[2]
    width = cotan.shape[2]
    slots = rows // micro
    shard_rows = out.shape[0]
    orders = axis_orders(digits)
    spans = row_spans(shard_rows)
    last = digits[2]
    per_row = width // LANES

    def masked(k):
        parts = []
        for b in range(micro):
            block = cotan_held[k, b * slots:(b + 1) * slots, :].astype(jnp.float32)
            place = lax.broadcasted_iota(jnp.int32, (slots, width), 0)
            parts.append(jnp.where(place < counts[b, k], block, 0.0))
        return parts[0] if micro == 1 else jnp.concatenate(parts, axis=0)

    steps3 = sorted(range(1, last[0]), key=lambda step: -min(step, last[0] - step)) + [0]
    piece = depth // pieces
    by_owner = pieces == lax.axis_size("dp")
    kinds = {"forward": [], "own": [], "mine": []}
    for step_a in range(digits[0][0]):
        for step_b in range(digits[1][0]):
            kind = "forward" if step_a and step_b else "own" if step_a or step_b else "mine"
            kinds[kind].append((step_a, step_b))
    groups = [("forward", 0), ("own", 0), ("forward", 1)]
    groups += [(kind, i) for i in range(len(steps3)) for kind in ("own", "forward", "mine") if (kind, i) not in groups]
    owners, places, group_of = [], [], {}
    for kind, i in groups:
        if i < len(steps3):
            group_of[kind, i] = range(len(owners), len(owners) + len(kinds[kind]))
            for step_a, step_b in kinds[kind]:
                places.append((step_a, step_b, steps3[i]))
                owners.append(dp + moved(step_a, digits[0]) + moved(step_b, digits[1]) + moved(steps3[i], last))
    if not by_owner:
        owners = list(range(pieces))

    def columns(at):
        start = owners[at] * piece
        return pl.ds(start if isinstance(start, int) else pl.multiple_of(start, LANES), piece)

    def to_mirror(src, dst, at):
        return pltpu.make_async_remote_copy(
            src_ref=src, dst_ref=dst, send_sem=part_send.at[at], recv_sem=part_recv.at[at],
            device_id=(dp, mirror), device_id_type=MESH)

    exchange = [to_mirror(acts_out.at[at], acts_in.at[at], at) for at in range(pieces)]
    exchange.append(to_mirror(cotan_out, cotan_in, pieces))
    loads[0].wait()
    cotan_out[...] = masked(1)
    rhs[0:rows, :] = masked(0).astype(jnp.bfloat16)
    loads[1].wait()
    for at in range(pieces):
        acts_out[at] = acts_held[1, :, columns(at)].astype(jnp.float32)
    pl.semaphore_wait(barrier, len(peers))
    exchange[pieces].start()
    for copy in exchange[:pieces]:
        copy.start()
    loads[2].wait()
    exchange[pieces].wait_recv()
    rhs[rows:2 * rows, :] = cotan_in[...].astype(jnp.bfloat16)

    def make(at):
        exchange[at].wait_recv()
        lhs = jnp.concatenate([acts_held[0, :, columns(at)], acts_in[at].astype(jnp.bfloat16)], axis=0)
        product = lax.dot_general(lhs, rhs[...], (((0,), (0,)), ((), ())), preferred_element_type=jnp.float32)
        first = owners[at] * (piece * per_row)
        if not isinstance(first, int):
            first = pl.multiple_of(first, 8)
        for c in range(per_row):
            grad[pl.ds(first + c, piece, stride=per_row), :] = product[:, c * LANES:(c + 1) * LANES]

    def make_group(kind, i):
        if by_owner and (kind, i) in group_of:
            for at in group_of.pop((kind, i)):
                make(at)
                made.append(places[at])

    made = []
    if not by_owner:
        for at in range(pieces):
            make(at)
        made += places

    def block(o, step1, step2, step3):
        first, second, third = orders[o]
        owner = dp + moved(step1, first) + moved(step2, second) + moved(step3, third)
        return grad.at[pl.ds(pl.multiple_of(owner * shard_rows + spans[o][0], 8), spans[o][1]), :]

    def base1(o, step1, step2, step3):
        first, second, third = orders[o]
        return ((step1 - 1) * second[0] + step2) * third[0] + step3

    def stage1(o, step1, step2, step3):
        at = base1(o, step1, step2, step3)
        return pltpu.make_async_remote_copy(
            src_ref=block(o, step1, step2, step3), dst_ref=got1[o].at[at], send_sem=send1[o].at[at], recv_sem=recv1[o].at[at],
            device_id=(dp + moved(step1, orders[o][0]), section), device_id_type=MESH)

    def stage2(o, step2, step3):
        at = (step2 - 1) * orders[o][2][0] + step3
        return pltpu.make_async_remote_copy(
            src_ref=block(o, 0, step2, step3), dst_ref=got2[o].at[at], send_sem=send2[o].at[at], recv_sem=recv2[o].at[at],
            device_id=(dp + moved(step2, orders[o][1]), section), device_id_type=MESH)

    def stage3(o, step3):
        at = step3 - 1
        return pltpu.make_async_remote_copy(
            src_ref=block(o, 0, 0, step3), dst_ref=got3[o].at[at], send_sem=send3[o].at[at], recv_sem=recv3[o].at[at],
            device_id=(dp + moved(step3, orders[o][2]), section), device_id_type=MESH)

    started = []

    def start(copy):
        copy.start()
        started.append(copy)

    def arrived1(o, step2, step3):
        total = block(o, 0, step2, step3)[...]
        for step1 in range(1, orders[o][0][0]):
            stage1(o, step1, step2, step3).wait_recv()
            total += got1[o][base1(o, step1, step2, step3)]
        return total

    def arrived2(o, step3):
        total = arrived1(o, 0, step3)
        for step2 in range(1, orders[o][1][0]):
            stage2(o, step2, step3).wait_recv()
            total += got2[o][(step2 - 1) * orders[o][2][0] + step3]
        return total

    def send_forward(i):
        if i < len(steps3):
            for o in range(2):
                for step1 in range(1, orders[o][0][0]):
                    for step2 in range(1, orders[o][1][0]):
                        start(stage1(o, step1, step2, steps3[i]))

    def send_own(i):
        if i < len(steps3):
            for o in range(2):
                for step1 in range(1, orders[o][0][0]):
                    start(stage1(o, step1, 0, steps3[i]))

    def send_second(i):
        for o in range(2):
            for step2 in range(1, orders[o][1][0]):
                block(o, 0, step2, steps3[i])[...] = arrived1(o, step2, steps3[i])
                start(stage2(o, step2, steps3[i]))

    def send_third(i):
        for o in range(2):
            block(o, 0, 0, steps3[i])[...] = arrived2(o, steps3[i])
            start(stage3(o, steps3[i]))

    late = range(2, len(spans))

    def late_first(step2, step3, step1):
        for o in late:
            if step1:
                start(stage1(o, step1, *((step2, step3) if orders[o][1] is digits[0] else (step3, step2))))

    def late_second():
        for o in late:
            for step2 in range(1, orders[o][1][0]):
                for step3 in reversed(range(orders[o][2][0])):
                    block(o, 0, step2, step3)[...] = arrived1(o, step2, step3)
                    start(stage2(o, step2, step3))

    def late_third():
        for o in late:
            for step3 in range(1, orders[o][2][0]):
                block(o, 0, 0, step3)[...] = arrived2(o, step3)
                start(stage3(o, step3))

    def send_late():
        while made:
            late_first(*made.pop(0))

    end = len(steps3) - 1
    make_group("forward", 0)
    send_forward(0)
    make_group("own", 0)
    send_own(0)
    send_late()
    make_group("forward", 1)
    if end > 1:
        send_forward(1)
    send_late()
    for kind, i in list(group_of):
        make_group(kind, i)
        send_late()
    for i in range(end + 1):
        if i == end and i:
            send_third(i - 1)
        send_second(i)
        if i == end - 1:
            send_forward(end)
        send_own(i + 1)
        if i + 2 < end:
            send_forward(i + 2)
        if 1 <= i < end:
            send_third(i - 1)
        if i == end - 2:
            late_second()
        if i == end - 1:
            late_third()
    if len(steps3) < 3:
        late_second()
    if len(steps3) < 2:
        late_third()
    for o in reversed(range(len(spans))):
        total = arrived2(o, 0)
        for step3 in range(1, orders[o][2][0]):
            stage3(o, step3).wait_recv()
            total += got3[o][step3 - 1]
        out[spans[o][0]:spans[o][0] + spans[o][1], :] = total
    for copy in exchange + started:
        copy.wait_send()


def shards(digits, acts, cotan, counts, weight, moment, second):
    micro = counts.shape[3]
    rows, depth = acts.shape[2], acts.shape[3]
    width = cotan.shape[3]
    shard_rows = weight.shape[1] // LANES
    piece = weight.shape[1] // width
    pieces = depth // piece if piece % LANES == 0 and weight.shape[1] % width == 0 else depth // (2 * LANES)
    orders = axis_orders(digits)
    spans = row_spans(shard_rows)
    orders = orders[:len(spans)]
    counts1 = [(first[0] - 1) * second[0] * third[0] for first, second, third in orders]
    counts2 = [(second[0] - 1) * third[0] for first, second, third in orders]
    counts3 = [third[0] - 1 for first, second, third in orders]

    def buffers(sizes):
        return [pltpu.VMEM((max(size, 1), span[1], LANES), jnp.float32) for size, span in zip(sizes, spans)]

    def semaphores(sizes):
        return [pltpu.SemaphoreType.DMA((max(size, 1),)) for size in sizes]

    hbm = pl.BlockSpec(memory_space=pl.ANY)
    vmem = pl.BlockSpec(memory_space=pltpu.VMEM)
    shard = pl.pallas_call(
        functools.partial(reduce_kernel, digits, micro, pieces),
        out_shape=jax.ShapeDtypeStruct((shard_rows, LANES), jnp.float32),
        in_specs=[hbm, hbm, pl.BlockSpec(memory_space=pltpu.SMEM)],
        out_specs=vmem,
        scratch_shapes=[
            pltpu.VMEM((2, rows, depth), jnp.bfloat16),
            pltpu.VMEM((2, rows, width), jnp.bfloat16),
            pltpu.VMEM((pieces, rows, depth // pieces), jnp.float32),
            pltpu.VMEM((rows, width), jnp.float32),
            pltpu.VMEM((pieces, rows, depth // pieces), jnp.float32),
            pltpu.VMEM((rows, width), jnp.float32),
            pltpu.VMEM((2 * rows, width), jnp.bfloat16),
            pltpu.VMEM((depth * width // LANES, LANES), jnp.float32),
            buffers(counts1), buffers(counts2), buffers(counts3),
            pltpu.SemaphoreType.DMA((3,)), pltpu.SemaphoreType.DMA((pieces + 1,)), pltpu.SemaphoreType.DMA((pieces + 1,)),
            semaphores(counts1), semaphores(counts1), semaphores(counts2), semaphores(counts2),
            semaphores(counts3), semaphores(counts3),
        ],
        compiler_params=pltpu.CompilerParams(collective_id=0, has_side_effects=True),
        name="reduce_grad",
    )(acts[0], cotan[0], counts[0, :, 0, :].T)
    flat = jax.ShapeDtypeStruct((shard_rows, LANES), jnp.float32)
    outs = pl.pallas_call(
        adamw_kernel,
        out_shape=(flat, flat, flat),
        in_specs=[vmem] * 4,
        out_specs=(vmem, vmem, vmem),
        name="adamw",
    )(shard, *(array.reshape(shard_rows, LANES) for array in (weight, moment, second)))
    return tuple(array.reshape(weight.shape) for array in outs)


AXES = {"A": (0, 1), "B": (1, 0), "C": (0, 1), "D": (1, 0)}


def flipped(family, first, second):
    return (first, second) if AXES[family][0] == 0 else (second, first)


def planes_beside(z, planes):
    return [p for p in (z - 1, z + 1) if 0 <= p < planes]


def crossed(c, place, z, planes):
    return tuple(("z", c, *place, z, p) for p in planes_beside(z, planes))


def toward(z, k):
    return 1 if k > z else -1


def third_needs(f, c, k, z):
    before = z - toward(z, k)
    return (("1", f, c, 0, k), ("2", f, c, k)) + ((("r", f, c, k, before),) if (before, k) in RELAYS else ())


def send_table(z, planes, spans):
    table = {}
    for f, c in spans[z]:
        if f in AXES:
            first, second = AXES[f]
        if f in "AB":
            for k in range(planes):
                for b in range(2):
                    table["1", f, c, b, k] = (first, z, (), flipped(f, 1, b) + (k,))
                table["2", f, c, k] = (second, z, (("1", f, c, 1, k),), flipped(f, 0, 1) + (k,))
                if k != z:
                    target = z + toward(z, k) if (z, k) in RELAYS else k
                    table["3", f, c, k] = (2, target, third_needs(f, c, k, z), (0, 0, k))
        elif f in "CD":
            for b in range(2):
                place = flipped(f, 1, b)
                table["x", f, c, b] = (first, z, crossed(c, place, z, planes), place + (z,))
            place = flipped(f, 0, 1)
            table["y", f, c] = (second, z, crossed(c, place, z, planes) + (("x", f, c, 1),), place + (z,))
        else:
            for k in range(planes):
                before = z - toward(z, k)
                for a in range(2 if k != z else 0):
                    for b in range(2):
                        needs = (("z", c, a, b, k, before),) if 0 <= before < planes else ()
                        table["z", c, a, b, k] = (2, z + toward(z, k), needs, (a, b, k))
    return table


def last_needs(f, c, z, planes):
    if f in "AB":
        return (("1", f, c, 0, z), ("2", f, c, z)) + tuple(("3", f, c, p) for p in range(planes) if p != z and (p, z) not in RELAYS)
    return crossed(c, (0, 0), z, planes) + (("x", f, c, 0), ("y", f, c))


def wait_groups(z, planes, spans):
    groups = []
    for f, c in spans[z]:
        if f in "AB":
            for k in range(planes):
                groups.append((("1", f, c, 1, k),))
                groups.append(third_needs(f, c, k, z) if k != z else last_needs(f, c, z, planes))
        elif f in "CD":
            groups += [(("x", f, c, 1),), (("x", f, c, 0), ("y", f, c))]
        else:
            for place in ((0, 0), (0, 1), (1, 0), (1, 1)):
                groups.append(crossed(c, place, z, planes))
                for k in range(planes):
                    before = z - toward(z, k)
                    if k != z and 0 <= before < planes:
                        groups.append((("z", c, *place, k, before),))
    return groups


def key_there(key, z):
    if key[0] == "3":
        return ("r",) + key[1:] + (z,) if (z, key[3]) in RELAYS else key[:-1] + (z,)
    return key + (z,) if key[0] == "z" else key


def span_of(key, spans, z, coming):
    if key[0] in "xy" or key[0] == "3" and coming:
        k = z
    else:
        k = key[4 if key[0] in "1z" else 3]
    return spans[k][("Z", key[1]) if key[0] == "z" else key[1:3]]


def spans_of(piece):
    planes = []
    for chunks in CHUNKS:
        total = sum(chunks["A"]) + sum(chunks["B"]) + sum(sum(pair) for pair in chunks["Z"])
        unit = piece // 8 // total * 8
        spans, at = {}, 0
        for f in "AB":
            for c, size in enumerate(chunks[f]):
                spans[f, c] = (at, size * unit)
                at += size * unit
        for c, (first, second) in enumerate(chunks["Z"]):
            spans["Z", c] = (at, (first + second) * unit)
            spans["C", c] = (at, first * unit)
            spans["D", c] = (at + first * unit, second * unit)
            at += (first + second) * unit
        planes.append(spans)
    return planes


def landing_of(z, planes, spans):
    places, at, groups = {}, 0, wait_groups(z, planes, spans)
    for i, group in enumerate(groups):
        for key in group:
            rows = span_of(key, spans, z, True)[1]
            places[key] = (at, rows, i)
            at += rows
    return places, groups, at


def part_groups(pieces):
    groups, at = [], 0
    for size in (1, 1, 1, 1, 2, 2):
        if at + size <= pieces:
            groups.append((at, size))
            at += size
    while at < pieces:
        groups.append((at, min(4, pieces - at)))
        at += groups[-1][1]
    return groups


def fast_kernel(digits, micro, acts, cotan, counts, weight, moment, second, packed, counts_held, acts_held, cotan_held,
                acts_out, cotan_out, acts_in, cotan_in, rhs, grad, got, state, shard, load_sem, part_send, part_recv,
                send_sem, recv_sem, up_sem):
    section = lax.axis_index("section")
    dp = lax.axis_index("dp")
    mirror = (dp, lax.axis_size("section") - 1 - section)
    planes = digits[2][0]
    strides = [stride for count, stride in digits]
    here = [lax.rem(lax.div(dp, stride), count) for count, stride in digits]
    across = [(1 - 2 * here[axis]) * strides[axis] for axis in range(2)]
    rows, depth = acts.shape[1], acts.shape[2]
    width = cotan.shape[2]
    slots = rows // micro
    pieces = lax.axis_size("dp")
    piece = depth // pieces
    per_row = width // LANES
    spans = spans_of(piece)
    tables = [send_table(z, planes, spans) for z in range(planes)]
    landings = [landing_of(z, planes, spans) for z in range(planes)]
    parts_in = part_groups(pieces)

    loads = [
        pltpu.make_async_copy(cotan, cotan_held, load_sem.at[0]),
        pltpu.make_async_copy(counts, counts_held, load_sem.at[1]),
        pltpu.make_async_copy(acts.at[1], acts_held.at[1], load_sem.at[2]),
        pltpu.make_async_copy(acts.at[0], acts_held.at[0], load_sem.at[3]),
    ]
    state_loads = [pltpu.make_async_copy(array, state.at[i], load_sem.at[4]) for i, array in enumerate((weight, moment, second))]
    for load in loads:
        load.start()

    barrier = pltpu.get_barrier_semaphore()
    pl.semaphore_signal(barrier, inc=1, device_id=mirror, device_id_type=MESH)
    for axis in range(2):
        @pl.when(here[axis] == 0)
        def greet():
            pl.semaphore_signal(barrier, inc=1, device_id=(dp + across[axis], section), device_id_type=MESH)
    for step in range(1, planes):
        @pl.when(here[2] + step < planes)
        def greet_plane():
            pl.semaphore_signal(barrier, inc=1, device_id=(dp + step * strides[2], section), device_id_type=MESH)

    def masked(k):
        parts = []
        for b in range(micro):
            block = cotan_held[k, b * slots:(b + 1) * slots, :].astype(jnp.float32)
            place = lax.broadcasted_iota(jnp.int32, (slots, width), 0)
            parts.append(jnp.where(place < counts_held[b, k], block, 0.0))
        return parts[0] if micro == 1 else jnp.concatenate(parts, axis=0)

    def to_mirror(src, dst, sent, received):
        return pltpu.make_async_remote_copy(
            src_ref=src, dst_ref=dst, send_sem=part_send.at[sent], recv_sem=part_recv.at[received],
            device_id=mirror, device_id_type=MESH)

    cotan_swap = to_mirror(cotan_out, cotan_in, 0, 0)
    group_at = {at + i: g for g, (at, size) in enumerate(parts_in) for i in range(size)}
    acts_swap = [to_mirror(acts_out.at[at], acts_in.at[at], 1, 1 + group_at[at]) for at in range(pieces)]
    loads[0].wait()
    loads[1].wait()
    cotan_out[...] = masked(1)
    pl.semaphore_wait(barrier, 1 + here[0] + here[1] + here[2])
    cotan_swap.start()
    rhs[0:rows, :] = masked(0).astype(jnp.bfloat16)
    for axis in range(2):
        @pl.when(here[axis] == 1)
        def answer():
            pl.semaphore_signal(up_sem.at[axis], inc=1, device_id=(dp + across[axis], section), device_id_type=MESH)
    for step in range(1, planes):
        @pl.when(here[2] >= step)
        def answer_plane():
            pl.semaphore_signal(up_sem.at[1 + step], inc=1, device_id=(dp - step * strides[2], section), device_id_type=MESH)
    loads[2].wait()

    def run(z):
        table = tables[z]
        places, groups, unused = landings[z]
        order = ORDERS[z]
        owners = []
        for key in order:
            if table[key][3] not in owners:
                owners.append(table[key][3])
        owners.append((0, 0, z))

        def owner_index(owner):
            return dp + owner[0] * across[0] + owner[1] * across[1] + (owner[2] - z) * strides[2]

        def columns(owner):
            return pl.ds(pl.multiple_of(owner_index(owner) * piece, LANES), piece)

        for at, owner in enumerate(owners):
            acts_out[at] = acts_held[1, :, columns(owner)].astype(jnp.float32)
            acts_swap[at].start()
        for load in state_loads:
            load.start()
        loads[3].wait()
        cotan_swap.wait_recv()
        rhs[rows:2 * rows, :] = cotan_in[...].astype(jnp.bfloat16)
        swapped = set()

        def make(at):
            g = group_at[at]
            if g not in swapped:
                swapped.add(g)
                part = acts_in.at[pl.ds(*parts_in[g])]
                to_mirror(part, part, 1, 1 + g).wait_recv()
            lhs = jnp.concatenate([acts_held[0, :, columns(owners[at])], acts_in[at].astype(jnp.bfloat16)], axis=0)
            first = pl.multiple_of(owner_index(owners[at]) * piece, piece)
            grad[pl.ds(first, piece), :] = lax.dot_general(
                lhs, rhs[...], (((0,), (0,)), ((), ())), preferred_element_type=jnp.float32)

        def block(owner, span):
            return pl.ds(pl.multiple_of(owner_index(owner) * piece + span[0], 8), span[1])

        def copy_of(key):
            axis, target, needs, owner = table[key]
            place, size, at = landings[target][0][key_there(key, z)]
            device = dp + across[axis] if axis < 2 else dp + (target - z) * strides[2]
            return pltpu.make_async_remote_copy(
                src_ref=grad.at[block(owner, span_of(key, spans, z, False)), :], dst_ref=got.at[pl.ds(place, size), :],
                send_sem=send_sem.at[0], recv_sem=recv_sem.at[at], device_id=(device, section), device_id_type=MESH)

        landed = set()

        def arrived(key, span):
            place, size, at = places[key]
            if at not in landed:
                landed.add(at)
                start = places[groups[at][0]][0]
                whole = got.at[pl.ds(start, sum(places[k][1] for k in groups[at])), :]
                pltpu.make_async_remote_copy(
                    src_ref=whole, dst_ref=whole, send_sem=send_sem.at[0], recv_sem=recv_sem.at[at],
                    device_id=mirror, device_id_type=MESH).wait_recv()
            place += span[0] - span_of(key, spans, z, True)[0]
            return got[place:place + span[1], :]

        met, done = set(), 0
        for key in order:
            axis, target, needs, owner = table[key]
            while done <= owners.index(owner):
                make(done)
                done += 1
            if needs:
                span = span_of(key, spans, z, False)
                at = block(owner, span)
                total = grad[at, :]
                for need in needs:
                    total += arrived(need, span)
                grad[at, :] = total
            if axis < 2 and axis not in met:
                met.add(axis)

                @pl.when(here[axis] == 0)
                def wait_up():
                    pl.semaphore_wait(up_sem.at[axis], 1)
            if axis == 2 and target > z and 1 + target - z not in met:
                met.add(1 + target - z)
                pl.semaphore_wait(up_sem.at[1 + target - z], 1)
            copy_of(key).start()
        for step in range(1, planes - z):
            if 1 + step not in met:
                pl.semaphore_wait(up_sem.at[1 + step], 1)
        while done < pieces:
            make(done)
            done += 1
        pltpu.make_async_copy(state, state, load_sem.at[4]).wait()
        for f, c in LASTS[z]:
            span = spans[z][f, c]
            total = grad[block((0, 0, z), span), :]
            for need in last_needs(f, c, z, planes):
                total += arrived(need, span)
            for part in range(per_row):
                shard[pl.ds(span[0] * per_row + part, span[1], stride=per_row), :] = total[:, part * LANES:(part + 1) * LANES]
            flat = slice(span[0] * per_row, (span[0] + span[1]) * per_row)
            updated = adamw_shard(shard[flat, :], state[0, flat, :], state[1, flat, :], state[2, flat, :])
            for i in range(3):
                packed[i, flat, :] = updated[i]
        cotan_swap.wait_send()
        to_mirror(acts_out, acts_in, 1, 1).wait_send()
        sent = grad.at[pl.ds(0, sum(span_of(key, spans, z, False)[1] for key in order)), :]
        pltpu.make_async_remote_copy(
            src_ref=sent, dst_ref=sent, send_sem=send_sem.at[0], recv_sem=recv_sem.at[0],
            device_id=mirror, device_id_type=MESH).wait_send()

    for z in range(planes):
        pl.when(here[2] == z)(functools.partial(run, z))


def put_kernel(packed, new_weight, new_moment, new_second, sem):
    copies = [pltpu.make_async_copy(packed.at[i], out, sem.at[i]) for i, out in enumerate((new_weight, new_moment, new_second))]
    for copy in copies:
        copy.start()
    for copy in copies:
        copy.wait()


def fast_fits(digits, acts, cotan, weight):
    planes, depth, width = digits[2][0], acts.shape[3], cotan.shape[3]
    piece = depth // (4 * planes)
    whole = all(sum(rows for (f, c), (at, rows) in spans.items() if f in "ABZ") == piece for spans in spans_of(piece))
    return (digits[0][0] == 2 and digits[1][0] == 2 and planes == len(ORDERS) and piece % LANES == 0 and whole
            and width % LANES == 0 and piece * width == weight.shape[1])


def fast_shards(digits, acts, cotan, counts, weight, moment, second):
    micro = counts.shape[3]
    rows, depth = acts.shape[2], acts.shape[3]
    width = cotan.shape[3]
    shard_rows = weight.shape[1] // LANES
    planes = digits[2][0]
    pieces = 4 * planes
    spans = spans_of(depth // pieces)
    landings = [landing_of(z, planes, spans) for z in range(planes)]
    received = max(len(groups) for places, groups, total in landings)
    space = max(total for places, groups, total in landings)
    hbm = pl.BlockSpec(memory_space=pl.ANY)
    vmem = pl.BlockSpec(memory_space=pltpu.VMEM)
    flat = (shard_rows, LANES)
    packed = pl.pallas_call(
        functools.partial(fast_kernel, digits, micro),
        out_shape=pltpu.VMEM((3, *flat), jnp.float32),
        in_specs=[hbm] * 6,
        out_specs=vmem,
        scratch_shapes=[
            pltpu.SMEM((micro, 2), jnp.int32),
            pltpu.VMEM((2, rows, depth), jnp.bfloat16),
            pltpu.VMEM((2, rows, width), jnp.bfloat16),
            pltpu.VMEM((pieces, rows, depth // pieces), jnp.float32),
            pltpu.VMEM((rows, width), jnp.float32),
            pltpu.VMEM((pieces, rows, depth // pieces), jnp.float32),
            pltpu.VMEM((rows, width), jnp.float32),
            pltpu.VMEM((2 * rows, width), jnp.bfloat16),
            pltpu.VMEM((depth, width), jnp.float32),
            pltpu.VMEM((space, width), jnp.float32),
            pltpu.VMEM((3, *flat), jnp.float32),
            pltpu.VMEM(flat, jnp.float32),
            pltpu.SemaphoreType.DMA((5,)), pltpu.SemaphoreType.DMA((2,)), pltpu.SemaphoreType.DMA((1 + len(part_groups(pieces)),)),
            pltpu.SemaphoreType.DMA((1,)), pltpu.SemaphoreType.DMA((received,)), pltpu.SemaphoreType.REGULAR((1 + planes,)),
        ],
        compiler_params=pltpu.CompilerParams(collective_id=0, has_side_effects=True, vmem_limit_bytes=66 * 10**6),
        name="reduce_adamw",
    )(acts[0], cotan[0], counts[0, :, 0, :].T, *(array.reshape(flat) for array in (weight, moment, second)))
    outs = pl.pallas_call(
        put_kernel,
        out_shape=(jax.ShapeDtypeStruct(flat, jnp.float32),) * 3,
        in_specs=[vmem],
        out_specs=(hbm, hbm, hbm),
        scratch_shapes=[pltpu.SemaphoreType.DMA((3,))],
        name="put",
    )(pltpu.with_memory_space_constraint(packed, pltpu.VMEM))
    return tuple(array.reshape(weight.shape) for array in outs)


def solution(mesh):
    in_specs = (
        P("section", None, "dp", None),
        P("section", None, "dp", None),
        P("section", None, "dp", None),
        P("section", "dp"),
        P("section", "dp"),
        P("section", "dp"),
    )
    out_specs = (P("section", "dp"), P("section", "dp"), P("section", "dp"))
    digits = dp_digits(mesh)

    def body(acts, cotan, counts, weight, moment, second):
        form = fast_shards if fast_fits(digits, acts, cotan, weight) else shards
        return form(digits, acts, cotan, counts, weight, moment, second)

    return jax.shard_map(body, mesh=mesh, in_specs=in_specs, out_specs=out_specs, check_vma=False)
```
